32 devices in a mesh: ctx: 16 (over z, x, core), ch: 2 (over y).
Axes of the slice: x: 2, y: 2, z: 4, core: 2. Of those that a mesh axis runs over, the one named last changes fastest.
Arguments:
- query: bfloat16 [4096, 2048], P('ch', 'ctx'), may hold values from -6 to 6
- key_in: bfloat16 [4096, 2048], P('ch', 'ctx'), may hold values from -6 to 6
- value_in: bfloat16 [4096, 2048], P('ch', 'ctx'), may hold values from -6 to 6
- grad_out: bfloat16 [4096, 2048], P('ch', 'ctx'), may hold values from -6 to 6
- med_filter: bfloat16 [256, 512], P('ch'), may hold values from -0.25 to 0.25
- residues: float32 [16, 256], P(None, 'ch'), may hold values from -4 to 4
- pole_rate: float32 [16, 256], P(None, 'ch'), may hold values from 0.05 to 400
Outputs:
- grad_query: bfloat16 [4096, 2048], P('ch', 'ctx')
- grad_key: bfloat16 [4096, 2048], P('ch', 'ctx')
- grad_value: bfloat16 [4096, 2048], P('ch', 'ctx')
- grad_med: float32 [256, 512], P('ch')
- grad_res: float32 [16, 256], P(None, 'ch')
The draws below stay inside these ranges and needn't reach their ends.
All inputs are finite; a program needn't handle non-finite values.
Results may differ from the reference program's by a relative error of at most 0.0055.
Values may be sent and summed in bfloat16 or wider, within the bound.
No kernel may reach another device: no remote copies, remote signals or barrier semaphores. Data moves between devices by JAX's collectives and lax.ppermute only.
A program may use at most 128 MiB of HBM per device.

```python
import math
import jax
import jax.numpy as jnp
from jax import lax

CHANNELS = 4096
GROUP = 16
GROUPS = 256
POLES = 16
BLK = 128
TOK_DEV = 128
TOKENS = 2048
MED = 512
N_CTX = 16


def level_of(rng, extent, pieces, least, top_value):
    def one(axis_at, blocks):
        draws = jax.random.uniform(jax.random.fold_in(jax.random.fold_in(rng, 6), axis_at), (blocks,), jnp.float32, least / len(pieces), top_value / len(pieces))
        return jnp.repeat(jnp.exp(draws), extent[axis_at] // blocks).reshape((-1,) + (1,) * (len(extent) - axis_at - 1))

    factor_of = one(*pieces[0])
    for cut in pieces[1:]:
        factor_of = factor_of * one(*cut)
    return factor_of


def noise(key, shape, spread, reach, cuts=(), dtype=jnp.bfloat16):
    level = level_of(key, shape, cuts, -0.22, 0.18) if cuts else 1.0
    entries = jax.random.normal(key, shape, jnp.float32) * spread * level
    return jnp.minimum(jnp.maximum(entries, -reach), reach).astype(dtype)


def setup_inputs(seed: int = 0) -> dict:
    key_list = jax.random.split(jax.random.key(seed), 8)
    return {
        "query": noise(key_list[0], (CHANNELS, TOKENS), 1.0, 6.0, ((0, 2), (1, 16))),
        "key_in": noise(key_list[1], (CHANNELS, TOKENS), 1.0, 6.0, ((0, 2), (1, 16))),
        "value_in": noise(key_list[2], (CHANNELS, TOKENS), 1.0, 6.0, ((0, 2), (1, 16))),
        "grad_out": noise(key_list[3], (CHANNELS, TOKENS), 1.0, 6.0, ((0, 2), (1, 16))),
        "med_filter": noise(key_list[4], (GROUPS, MED), MED ** -0.5, 0.25, ((0, 2),)),
        "residues": noise(key_list[5], (POLES, GROUPS), 1.0, 4.0, ((1, 2),), jnp.float32),
        "pole_rate": jnp.clip(jnp.exp(math.log(400.0) - 8.987197 * jax.random.uniform(key_list[6], (POLES, GROUPS), jnp.float32) ** level_of(key_list[6], (POLES, GROUPS), ((1, 2),), -0.2, 0.2)), 0.05, 400.0),
    }


def contract(formula, left, right):
    return jnp.einsum(formula, left.astype(jnp.float32), right.astype(jnp.float32))

def exact_reduction(formula, left, right):
    return jnp.einsum(formula, left, right, precision=lax.Precision.HIGHEST)

def build_tables(padded, offset, block_size):
    segment = lax.dynamic_slice_in_dim(padded, offset * block_size, 2 * block_size, 1)
    places = jnp.arange(block_size)
    lookup = block_size + places[None, :] - places[:, None]
    return segment[:, lookup]

def diag_sums(tile_sums):
    groups, block_size = (tile_sums.shape[0], tile_sums.shape[1])
    flipped = tile_sums[:, ::-1, :]
    widened = jnp.pad(flipped, ((0, 0), (0, 0), (0, block_size)))
    flattened = widened.reshape(groups, 2 * block_size * block_size)[:, :2 * block_size * block_size - block_size]
    return lax.optimization_barrier(jnp.sum(flattened.reshape(groups, block_size, 2 * block_size - 1), axis=1))

def three_ways(earlier, following, filters, offsets, block_size, out_len):
    groups, members = (earlier.shape[0], earlier.shape[1])
    padding_len = (offsets - 1) * block_size
    earlier = jnp.pad(earlier, ((0, 0), (0, 0), (padding_len - (earlier.shape[2] - out_len), 0)))
    following = jnp.pad(following, ((0, 0), (0, 0), (0, padding_len - (following.shape[2] - out_len))))
    out_blocks = out_len // block_size
    all_blocks = out_blocks + offsets - 1
    early_blocks = earlier.reshape(groups, members, all_blocks, block_size)
    late_blocks = following.reshape(groups, members, all_blocks, block_size)
    own_late = late_blocks[:, :, :out_blocks]
    lag_count = filters.shape[1]
    padded = jnp.pad(filters, ((0, 0), (block_size, 2 * block_size)))

    def one_turn(offset, carry):
        forward, backward, accumulated = carry
        offset = offset.astype(jnp.int32)
        tables = build_tables(padded, offset, block_size)
        source = lax.dynamic_slice_in_dim(early_blocks, offsets - 1 - offset, out_blocks, 2)
        upcoming = lax.dynamic_slice_in_dim(late_blocks, offset, out_blocks, 2)
        forward = forward + contract('gcib,gba->gcia', source, tables)
        backward = backward + contract('gcjb,gab->gcja', upcoming, tables)
        tile_sums = contract('gcib,gcia->gba', source, own_late)
        anchor = offset * block_size + 1
        window = lax.dynamic_slice_in_dim(accumulated, anchor, 2 * block_size - 1, 1)
        accumulated = lax.dynamic_update_slice_in_dim(accumulated, window + diag_sums(tile_sums), anchor, 1)
        return (forward, backward, accumulated)
    initial = (jnp.zeros((groups, members, out_blocks, block_size), jnp.float32), jnp.zeros((groups, members, out_blocks, block_size), jnp.float32), jnp.zeros((groups, lag_count + 3 * block_size), jnp.float32))
    forward, backward, accumulated = lax.fori_loop(0, offsets, one_turn, initial)
    return (forward.reshape(groups, members, out_len), backward.reshape(groups, members, out_len), accumulated[:, block_size:block_size + lag_count])

def reference(query, key_in, value_in, grad_out, med_filter, residues, pole_rate):
    groups = CHANNELS // GROUP
    product = (key_in.astype(jnp.float32) * value_in.astype(jnp.float32)).astype(jnp.bfloat16)
    gated = (grad_out.astype(jnp.float32) * query.astype(jnp.float32)).astype(jnp.bfloat16)
    prod_three = product.reshape(groups, GROUP, TOKENS)
    gate_three = gated.reshape(groups, GROUP, TOKENS)
    earlier = jnp.pad(prod_three, ((0, 0), (0, 0), (MED, 0)))
    following = jnp.pad(gate_three, ((0, 0), (0, 0), (0, MED)))
    med_out, med_back, med_grad = three_ways(earlier, following, med_filter, MED // BLK + 1, BLK, TOKENS)
    decay_rate = pole_rate.T
    gain_root = jnp.sqrt(-jnp.expm1(-2.0 * decay_rate / TOKENS))
    residue_factor = residues.T * gain_root
    lag_values = jnp.arange(TOK_DEV).astype(jnp.float32)
    powers = jnp.exp(-decay_rate[:, :, None] * lag_values / TOKENS)
    long_table = lax.optimization_barrier(jnp.sum(residue_factor[:, :, None] * powers, axis=1)).astype(jnp.bfloat16)
    seg_prod = prod_three.reshape(groups, GROUP * N_CTX, TOK_DEV)
    seg_gate = gate_three.reshape(groups, GROUP * N_CTX, TOK_DEV)
    long_out, long_back, long_grad = three_ways(seg_prod, seg_gate, long_table, TOK_DEV // BLK, BLK, TOK_DEV)
    decay_final = jnp.exp(-decay_rate[:, None, :] * (TOK_DEV - 1.0 - lag_values)[None, :, None] / TOKENS)
    decay_initial = jnp.exp(-decay_rate[:, :, None] * (lag_values + 1.0) / TOKENS)
    prod_four = prod_three.reshape(groups, GROUP, N_CTX, TOK_DEV).astype(jnp.float32)
    gate_four = gate_three.reshape(groups, GROUP, N_CTX, TOK_DEV).astype(jnp.float32)
    final_state = exact_reduction('gcks,gsp->gckp', prod_four, decay_final)
    leading_state = exact_reduction('gckt,gpt->gckp', gate_four, decay_initial)
    block_decay = jnp.exp(-decay_rate * TOK_DEV / TOKENS)[:, None, :]

    def advance(states, incoming):
        return (states * block_decay + incoming, states)
    zero_state = jnp.zeros((groups, GROUP, POLES), jnp.float32)
    unused_one, carried_over = lax.scan(advance, zero_state, jnp.moveaxis(final_state, 2, 0))
    unused_two, returned_state = lax.scan(advance, zero_state, jnp.moveaxis(leading_state, 2, 0), reverse=True)
    carried_over = jnp.moveaxis(carried_over, 0, 2)
    returned_state = jnp.moveaxis(returned_state, 0, 2)
    cross_output = exact_reduction('gckp,gpt->gckt', carried_over, residue_factor[:, :, None] * decay_initial)
    cross_gradient = exact_reduction('gckp,gsp->gcks', returned_state, residue_factor[:, None, :] * decay_final)
    conv_out = med_out + long_out.reshape(groups, GROUP, TOKENS) + cross_output.reshape(groups, GROUP, TOKENS)
    input_grad = med_back + long_back.reshape(groups, GROUP, TOKENS) + cross_gradient.reshape(groups, GROUP, TOKENS)
    conv_out = conv_out.reshape(CHANNELS, TOKENS)
    input_grad = input_grad.reshape(CHANNELS, TOKENS)
    grad_query = (grad_out.astype(jnp.float32) * conv_out).astype(jnp.bfloat16)
    grad_key = (input_grad * value_in.astype(jnp.float32)).astype(jnp.bfloat16)
    grad_value = (input_grad * key_in.astype(jnp.float32)).astype(jnp.bfloat16)
    scaling = 1.0 / math.sqrt(GROUP * TOKENS)
    grad_med = med_grad * scaling
    cross_coef = lax.optimization_barrier(jnp.sum(leading_state * carried_over, axis=(1, 2)))
    intra_coef = exact_reduction('gl,gpl->gp', long_grad, powers)
    grad_res = ((intra_coef + cross_coef) * gain_root * scaling).T
    return (grad_query, grad_key, grad_value, grad_med, grad_res)
```

```python
import functools
import math

import jax
import jax.numpy as jnp
from jax import lax
from jax.experimental import pallas as pl
from jax.experimental.pallas import tpu as pltpu
from jax.sharding import PartitionSpec as P

GROUP = 16
BLK = 128
SPAN = 4
STEP = 8
WIDE = (SPAN + 1) * BLK
F32 = jnp.float32
BF16 = jnp.bfloat16
NT = (((1,), (1,)), ((), ()))
TN = (((0,), (0,)), ((), ()))
NN = (((1,), (0,)), ((), ()))


def mm(left, right, dims=NN):
    return lax.dot_general(left, right, dims, preferred_element_type=F32)


def halves(value):
    high = value.astype(BF16)
    return high, (value - high.astype(F32)).astype(BF16)


def lanes_of(rows):
    return lax.broadcasted_iota(jnp.int32, (rows, BLK), 1)


def table_kernel(rate_ref, gain_ref, med_ref, table_ref):
    lane = lanes_of(GROUP).astype(F32)
    for g in range(STEP):
        rate = rate_ref[g]
        gain = gain_ref[g]
        pieces = [jnp.zeros((1, BLK), F32)]
        for o in range(SPAN + 1):
            tail = jnp.sum(gain * jnp.exp(-rate * (lane + float(o * BLK))), axis=0, keepdims=True)
            if o < SPAN:
                tail = tail + med_ref[g : g + 1, o * BLK : (o + 1) * BLK].astype(F32)
            pieces.append(tail)
        taps = jnp.broadcast_to(jnp.concatenate(pieces, axis=1), (GROUP, WIDE + BLK))
        skewed = pltpu.roll(taps, 0, 1, stride=1, stride_axis=0)
        for i in range(BLK // GROUP):
            moved = skewed if i == 0 else pltpu.roll(skewed, GROUP * i, 1)
            table_ref[g, GROUP * i : GROUP * (i + 1), :] = moved[:, BLK:].astype(BF16)


def state_kernel(q_ref, rate_ref, p0, p1, p2, p3, end_ref, head_ref, both):
    q = q_ref[0]
    lane = lanes_of(GROUP)
    tok = lane.astype(F32)
    for m, piece in enumerate((p0, p1, p2, p3)):
        both[q ^ m] = piece[...]
    ends = jnp.zeros((GROUP, BLK), F32)
    heads = jnp.zeros((GROUP, BLK), F32)
    for g in range(STEP):
        rate = rate_ref[g]
        rows = slice(GROUP * g, GROUP * (g + 1))
        own = jnp.concatenate(
            [both[s, 0, rows, :] for s in range(SPAN)] + [both[s, 1, rows, :] for s in range(SPAN)],
            axis=0,
        )
        fin = halves(jnp.exp(-rate * (BLK - 1.0 - tok)))
        ini = halves(jnp.exp(-rate * (tok + 1.0)))
        state = mm(jnp.concatenate(fin + ini, axis=0), own, NT)
        end = state[0:16] + state[16:32]
        head = state[32:48] + state[48:64]
        block = (lane // GROUP).astype(F32)
        end = jnp.where(lane < 64, end * jnp.exp(-rate * (BLK * (SPAN - 1.0 - block))), 0.0)
        head = jnp.where(lane >= 64, head * jnp.exp(-rate * (BLK * (block - SPAN))), 0.0)
        for value, is_end in ((end, True), (head, False)):
            value = value + pltpu.roll(value, 64, 1)
            value = value + pltpu.roll(value, 32, 1)
            value = value + pltpu.roll(value, 16, 1)
            if is_end:
                ends = jnp.where(lane // GROUP == g, value, ends)
            else:
                heads = jnp.where(lane // GROUP == g, value, heads)
    end_ref[0] = ends
    head_ref[0] = heads


def roll_left(value, amount):
    width = value.shape[1]
    return value if amount % width == 0 else pltpu.roll(value, width - amount, 1)


def main_kernel(
    q_ref, rate_ref, gain_ref, table_ref, before_ref, after_ref,
    p0, p1, p2, p3, xa, xb, ga, gb,
    o0, o1, o2, o3, lag_ref, res_ref, xs, gs, fs, bs,
):
    q = q_ref[0]
    lane = lanes_of(GROUP)
    tok = lane.astype(F32)
    block = lane // GROUP
    for m, piece in enumerate((p0, p1, p2, p3)):
        xs[SPAN + (q ^ m)] = piece[0]
        gs[q ^ m] = piece[1]
    for m, (x_part, g_part) in enumerate(((xa, ga), (xa, ga), (xb, gb), (xb, gb))):
        xs[q ^ m] = x_part[m % 2]
        gs[SPAN + (q ^ m)] = g_part[m % 2]
    row_at = lax.broadcasted_iota(jnp.int32, (BLK, BLK), 0)
    col_at = lax.broadcasted_iota(jnp.int32, (BLK, BLK), 1)
    causal = col_at >= row_at
    sub_at = lax.broadcasted_iota(jnp.int32, (8, WIDE), 0)
    lag_rows = []
    for g in range(STEP):
        rate = rate_ref[g]
        gain = gain_ref[g]
        rows = slice(GROUP * g, GROUP * (g + 1))
        x = [xs[j, rows, :] for j in range(2 * SPAN)]
        y = [gs[j, rows, :] for j in range(2 * SPAN)]
        fin = jnp.exp(-rate * (BLK - 1.0 - tok))
        ini = jnp.exp(-rate * (tok + 1.0))
        end = mm(jnp.concatenate(halves(fin), axis=0), jnp.concatenate(x, axis=0), NT)
        end = end[0:16] + end[16:32]
        head = mm(jnp.concatenate(halves(ini), axis=0), jnp.concatenate(y, axis=0), NT)
        head = head[0:16] + head[16:32]

        def spread(ref):
            start = jnp.where(lane < GROUP, roll_left(ref[0], GROUP * g), 0.0)
            start = start + pltpu.roll(start, 16, 1)
            return start + pltpu.roll(start, 32, 1)

        decay = [jnp.exp(-rate * float(BLK * k)) for k in range(SPAN)]
        near = block.astype(F32)
        carried = spread(before_ref) * jnp.exp(-rate * (BLK * near))
        returned = spread(after_ref) * jnp.exp(-rate * (BLK * (SPAN - 1.0 - near)))
        for k in range(SPAN - 1):
            moved = pltpu.roll(end, GROUP * (k + 1), 1)
            moved = jnp.where(lane >= GROUP * (k + 1), moved, 0.0)
            carried = carried + (moved if k == 0 else moved * decay[k])
            moved = pltpu.roll(head, GROUP * (SPAN - 1 - k), 1)
            moved = jnp.where(lane < GROUP * (SPAN - 1 - k), moved, 0.0)
            returned = returned + (moved if k == 0 else moved * decay[k])
        skip = jnp.exp(-rate * float(SPAN * BLK))
        cross = jnp.where(lane < 64, pltpu.roll(end, 64, 1) * returned * skip, 0.0)
        out_f = halves(gain * ini * skip)
        out_b = halves(gain * fin * skip)
        car = halves(carried[:, :64])
        ret = halves(returned[:, :64])
        far_f = mm(
            jnp.concatenate((car[0], car[1], car[0]), axis=0),
            jnp.concatenate((out_f[0], out_f[0], out_f[1]), axis=0),
            TN,
        )
        far_b = mm(
            jnp.concatenate((ret[0], ret[1], ret[0]), axis=0),
            jnp.concatenate((out_b[0], out_b[0], out_b[1]), axis=0),
            TN,
        )
        wide_x = jnp.concatenate(
            [jnp.concatenate(x[SPAN - o : 2 * SPAN - o], axis=0) for o in range(SPAN + 1)], axis=1
        )
        wide_y = jnp.concatenate(
            [jnp.concatenate(y[o : o + SPAN], axis=0) for o in range(SPAN + 1)], axis=1
        )
        table = table_ref[g]
        tall = jnp.concatenate(
            [table[:, o * BLK : (o + 1) * BLK] for o in range(SPAN + 1)], axis=0
        )
        forward = mm(wide_x, tall) + far_f
        backward = mm(wide_y, table, NT) + far_b
        for i in range(SPAN):
            fs[i, rows, :] = forward[GROUP * i : GROUP * (i + 1)].astype(BF16)
            bs[i, rows, :] = backward[GROUP * i : GROUP * (i + 1)].astype(BF16)
        own_x = jnp.concatenate(x[SPAN:], axis=0)
        pairs = mm(own_x, wide_y, TN)
        pairs = jnp.concatenate((jnp.where(causal, pairs[:, :BLK], 0.0), pairs[:, BLK:]), axis=1)
        total = pairs[0:8]
        for i in range(1, BLK // 8):
            total = total + roll_left(pairs[8 * i : 8 * (i + 1)], 8 * i)
        for bit in (1, 2, 4):
            total = jnp.where((sub_at & bit) != 0, roll_left(total, bit), total)
        lags = jnp.sum(total, axis=0, keepdims=True)
        lag_rows.append(lags)
        for o in range(SPAN + 1):
            cross = cross + lags[:, o * BLK : (o + 1) * BLK] * jnp.exp(
                -rate * (tok + float(o * BLK))
            )
        res_ref[g] = cross
    lag_ref[...] = jnp.concatenate(lag_rows, axis=0)
    for m, out in enumerate((o0, o1, o2, o3)):
        out[0] = fs[q ^ m]
        out[1] = bs[q ^ m]


def gate_kernel(q_ref, p0, p1, p2, p3, go_ref, v_ref, k_ref, gq_ref, gk_ref, gv_ref):
    q = q_ref[0]
    sub = p0.shape[1]
    for m, piece in enumerate((p0, p1, p2, p3)):
        at = pl.ds(pl.multiple_of((q ^ m) * sub, sub), sub)
        gq_ref[at, :] = (go_ref[at, :].astype(F32) * piece[0].astype(F32)).astype(BF16)
        grad = piece[1].astype(F32)
        gk_ref[at, :] = (grad * v_ref[at, :].astype(F32)).astype(BF16)
        gv_ref[at, :] = (grad * k_ref[at, :].astype(F32)).astype(BF16)


def body(query, key_in, value_in, grad_out, med_filter, residues, pole_rate):
    channels, length = query.shape
    groups = channels // GROUP
    devices = lax.axis_size("ctx")
    seq_total = length * devices
    ranks = SPAN
    units = devices // ranks
    sub = channels // ranks
    local = groups // ranks
    index = lax.axis_index("ctx")
    q = lax.rem(index, ranks).astype(jnp.int32)
    q_arr = q.reshape(1)

    def swap(value, m):
        return lax.ppermute(value, "ctx", [(i, i ^ m) for i in range(devices)])

    def shift(value, by):
        by = by * ranks
        return lax.ppermute(
            value, "ctx", [(i, i + by) for i in range(devices) if 0 <= i + by < devices]
        )

    def part(m):
        def cut(array):
            return lax.dynamic_slice_in_dim(array, (q ^ m) * sub, sub, 0).astype(F32)

        return jnp.stack(
            [
                (cut(key_in) * cut(value_in)).astype(BF16),
                (cut(grad_out) * cut(query)).astype(BF16),
            ]
        )

    pieces = [part(0)] + [swap(part(m), m) for m in range(1, ranks)]

    x_near = shift(jnp.stack([pieces[0][0], pieces[1][0]]), 1)
    y_near = shift(jnp.stack([pieces[0][1], pieces[1][1]]), -1)
    x_far = shift(jnp.stack([pieces[2][0], pieces[3][0]]), 1)
    y_far = shift(jnp.stack([pieces[2][1], pieces[3][1]]), -1)

    rate = lax.dynamic_slice_in_dim(pole_rate, q * local, local, 1).T / seq_total
    res = lax.dynamic_slice_in_dim(residues, q * local, local, 1).T
    med = lax.dynamic_slice_in_dim(med_filter, q * local, local, 0)
    root = jnp.sqrt(-jnp.expm1(-2.0 * rate))
    rate_wide = jnp.broadcast_to(rate[:, :, None], (local, GROUP, BLK))
    gain_wide = jnp.broadcast_to((res * root)[:, :, None], (local, GROUP, BLK))

    steps = local // STEP
    smem = pl.BlockSpec(memory_space=pltpu.SMEM)
    per_group = pl.BlockSpec((STEP, GROUP, BLK), lambda i: (i, 0, 0))
    packed = pl.BlockSpec((1, GROUP, BLK), lambda i: (i, 0, 0))
    rows = STEP * GROUP
    pair = pl.BlockSpec((2, rows, BLK), lambda i: (0, i, 0))
    params = pltpu.CompilerParams(vmem_limit_bytes=40 << 20)

    table = pl.pallas_call(
        table_kernel,
        grid=(steps,),
        in_specs=[per_group, per_group, pl.BlockSpec((STEP, SPAN * BLK), lambda i: (i, 0))],
        out_specs=pl.BlockSpec((STEP, BLK, WIDE), lambda i: (i, 0, 0)),
        out_shape=jax.ShapeDtypeStruct((local, BLK, WIDE), BF16),
        compiler_params=params,
        name="tables",
    )(rate_wide, gain_wide, med)

    ends, heads = pl.pallas_call(
        state_kernel,
        grid=(steps,),
        in_specs=[smem, per_group] + [pair] * 4,
        out_specs=[packed] * 2,
        out_shape=[jax.ShapeDtypeStruct((steps, GROUP, BLK), F32)] * 2,
        scratch_shapes=[pltpu.VMEM((SPAN, 2, rows, BLK), BF16)],
        compiler_params=params,
        name="states",
    )(q_arr, rate_wide, *pieces)

    rate_packed = jnp.repeat(
        jnp.transpose(rate.reshape(steps, STEP, GROUP), (0, 2, 1)), GROUP, axis=2
    )
    reach = 1
    while reach < units - 2:
        fade = jnp.exp(-rate_packed * float(reach * ranks * length))
        ends, heads = ends + fade * shift(ends, reach), heads + fade * shift(heads, -reach)
        reach *= 2
    before = shift(ends, 2)
    after = shift(heads, -2)

    outs = pl.pallas_call(
        main_kernel,
        grid=(steps,),
        in_specs=[
            smem,
            per_group,
            per_group,
            pl.BlockSpec((STEP, BLK, WIDE), lambda i: (i, 0, 0)),
            packed,
            packed,
        ]
        + [pair] * 8,
        out_specs=[pair] * 4 + [pl.BlockSpec((STEP, WIDE), lambda i: (i, 0)), per_group],
        out_shape=[jax.ShapeDtypeStruct((2, sub, BLK), BF16)] * 4
        + [
            jax.ShapeDtypeStruct((local, WIDE), F32),
            jax.ShapeDtypeStruct((local, GROUP, BLK), F32),
        ],
        scratch_shapes=[pltpu.VMEM((2 * SPAN, rows, BLK), BF16)] * 2
        + [pltpu.VMEM((SPAN, rows, BLK), BF16)] * 2,
        compiler_params=params,
        name="convs",
    )(q_arr, rate_wide, gain_wide, table, before, after, *pieces, x_near, x_far, y_near, y_far)

    back = [outs[0]] + [swap(outs[m], m) for m in range(1, ranks)]
    whole = pl.BlockSpec(memory_space=pltpu.VMEM)
    grads = pl.pallas_call(
        gate_kernel,
        in_specs=[smem] + [whole] * 7,
        out_specs=[whole] * 3,
        out_shape=[jax.ShapeDtypeStruct((channels, length), BF16)] * 3,
        compiler_params=params,
        name="gates",
    )(q_arr, *back, grad_out, value_in, key_in)

    scaling = 1.0 / math.sqrt(GROUP * seq_total)
    terms = jnp.sum(outs[5], axis=2) * root
    sums = jnp.concatenate([outs[4][:, : SPAN * BLK], terms], axis=1) * scaling
    hop = 1
    while hop < units:
        sums = sums + swap(sums, hop * ranks)
        hop *= 2
    gathered = jnp.zeros((groups, sums.shape[1]), F32)
    for m in range(ranks):
        got = sums if m == 0 else swap(sums, m)
        gathered = lax.dynamic_update_slice_in_dim(gathered, got, (q ^ m) * local, 0)
    return (
        grads[0],
        grads[1],
        grads[2],
        gathered[:, : SPAN * BLK],
        gathered[:, SPAN * BLK :].T,
    )


def solution(mesh):
    in_specs = (
        P("ch", "ctx"),
        P("ch", "ctx"),
        P("ch", "ctx"),
        P("ch", "ctx"),
        P("ch", None),
        P(None, "ch"),
        P(None, "ch"),
    )
    out_specs = (P("ch", "ctx"), P("ch", "ctx"), P("ch", "ctx"), P("ch", None), P(None, "ch"))
    return jax.shard_map(body, mesh=mesh, in_specs=in_specs, out_specs=out_specs, check_vma=False)
```

```python
import functools
import math

import jax
import jax.numpy as jnp
from jax import lax
from jax.experimental import pallas as pl
from jax.experimental.pallas import tpu as pltpu
from jax.sharding import PartitionSpec as P

GROUP = 16
BLK = 128
SPAN = 4
STEP = 8
PARTS = 2
WIDE = (SPAN + 1) * BLK
F32 = jnp.float32
BF16 = jnp.bfloat16
NT = (((1,), (1,)), ((), ()))
TN = (((0,), (0,)), ((), ()))
NN = (((1,), (0,)), ((), ()))


def mm(left, right, dims=NN):
    return lax.dot_general(left, right, dims, preferred_element_type=F32)


def halves(value):
    high = value.astype(BF16)
    return high, (value - high.astype(F32)).astype(BF16)


def lanes_of(rows):
    return lax.broadcasted_iota(jnp.int32, (rows, BLK), 1)


def table_kernel(rate_ref, gain_ref, med_ref, table_ref):
    lane = lanes_of(GROUP).astype(F32)
    for g in range(STEP):
        rate = rate_ref[g]
        gain = gain_ref[g]
        pieces = [jnp.zeros((1, BLK), F32)]
        for o in range(SPAN + 1):
            tail = jnp.sum(gain * jnp.exp(-rate * (lane + float(o * BLK))), axis=0, keepdims=True)
            if o < SPAN:
                tail = tail + med_ref[g : g + 1, o * BLK : (o + 1) * BLK].astype(F32)
            pieces.append(tail)
        taps = jnp.broadcast_to(jnp.concatenate(pieces, axis=1), (GROUP, WIDE + BLK))
        skewed = pltpu.roll(taps, 0, 1, stride=1, stride_axis=0)
        for i in range(BLK // GROUP):
            moved = skewed if i == 0 else pltpu.roll(skewed, GROUP * i, 1)
            table_ref[g, GROUP * i : GROUP * (i + 1), :] = moved[:, BLK:].astype(BF16)


def own_group(rows):
    row = lax.broadcasted_iota(jnp.int32, (rows, BLK), 0) // (rows // STEP)
    return row == lax.broadcasted_iota(jnp.int32, (rows, BLK), 1) // GROUP


def column_sum(value):
    total = value[0:GROUP]
    for g in range(1, STEP):
        total = total + value[GROUP * g : GROUP * (g + 1)]
    return total


def gather_blocks(q, pieces, near, far, xs, ys):
    for m, piece in enumerate(pieces):
        xs[SPAN + (q ^ m)] = piece[0]
        ys[q ^ m] = piece[1]
    for m in range(SPAN):
        x_part, y_part = near if m < 2 else far
        xs[q ^ m] = x_part[m % 2]
        ys[SPAN + (q ^ m)] = y_part[m % 2]


def state_kernel(
    q_ref, rate_ref, row_ref, p0, p1, p2, p3, xa, xb, ya, yb,
    car_ref, ret_ref, end_ref, ahead_ref, behind_ref, cross_ref, xs, ys,
):
    gather_blocks(q_ref[0], (p0, p1, p2, p3), (xa, ya), (xb, yb), xs, ys)
    rate = rate_ref[...].reshape(BLK, BLK)
    tok = lanes_of(BLK).astype(F32)
    row = row_ref[0, 0:1, :]
    decay = jnp.exp(-row * float(BLK))
    skip = jnp.exp(-row * float(SPAN * BLK))
    same = own_group(BLK)
    fin = jnp.concatenate(halves(jnp.exp(-rate * (BLK - 1.0 - tok))), axis=0)
    ini = jnp.concatenate(halves(jnp.exp(-rate * (tok + 1.0))), axis=0)

    def state(blocks, j, weights):
        both = mm(blocks[j], weights, NT)
        return jnp.where(same, both[:, :BLK] + both[:, BLK:], 0.0)

    carried = state(xs, 0, fin)
    for i in range(1, SPAN):
        car_ref[0, i - 1] = carried.astype(BF16)
        carried = carried * decay + state(xs, i, fin)
    own = [state(xs, SPAN + i, fin) for i in range(SPAN)]
    end = own[0]
    for i in range(1, SPAN):
        end = end * decay + own[i]
    end_ref[0] = column_sum(end)
    ahead_ref[0] = column_sum(end + skip * carried)

    returned = state(ys, 2 * SPAN - 1, ini)
    cross = jnp.zeros((BLK, BLK), F32)
    for i in range(SPAN - 2, -1, -1):
        ret_ref[0, i] = returned.astype(BF16)
        cross = cross + own[i] * returned
        returned = returned * decay + state(ys, SPAN + i, ini)
    head = state(ys, SPAN - 1, ini)
    for i in range(SPAN - 2, -1, -1):
        head = head * decay + state(ys, i, ini)
    behind_ref[0] = column_sum(head + skip * returned)
    cross_ref[0] = column_sum(cross) * skip


def roll_left(value, amount):
    width = value.shape[1]
    return value if amount % width == 0 else pltpu.roll(value, width - amount, 1)


def fold(value):
    for step in (64, 32, 16):
        value = value + pltpu.roll(value, step, 1)
    return value


def lag_kernel(
    q_ref, rate_ref, row_ref, root_ref, cross_ref, p0, p1, p2, p3, ya, yb, lag_ref, xs, ys,
    *, scale,
):
    q = q_ref[0]
    for m, piece in enumerate((p0, p1, p2, p3)):
        xs[q ^ m] = piece[0]
        ys[q ^ m] = piece[1]
        ys[SPAN + (q ^ m)] = (ya if m < 2 else yb)[m % 2]
    row_at = lax.broadcasted_iota(jnp.int32, (BLK, BLK), 0)
    causal = lanes_of(BLK) >= row_at
    sub_at = lax.broadcasted_iota(jnp.int32, (8, WIDE), 0)
    lag_rows = []
    for g in range(STEP):
        rows = slice(GROUP * g, GROUP * (g + 1))
        y = [ys[j, rows, :] for j in range(2 * SPAN)]
        wide_y = jnp.concatenate(
            [jnp.concatenate(y[o : o + SPAN], axis=0) for o in range(SPAN + 1)], axis=1
        )
        own_x = jnp.concatenate([xs[j, rows, :] for j in range(SPAN)], axis=0)
        pairs = mm(own_x, wide_y, TN)
        pairs = jnp.concatenate((jnp.where(causal, pairs[:, :BLK], 0.0), pairs[:, BLK:]), axis=1)
        total = pairs[0:8]
        for i in range(1, BLK // 8):
            total = total + roll_left(pairs[8 * i : 8 * (i + 1)], 8 * i)
        for bit in (1, 2, 4):
            total = jnp.where((sub_at & bit) != 0, roll_left(total, bit), total)
        lag_rows.append(jnp.sum(total, axis=0, keepdims=True))
    lags = jnp.concatenate(lag_rows, axis=0)
    rate = rate_ref[...].reshape(BLK, BLK)
    row = row_ref[0, 0:1, :]
    fade = jnp.concatenate(halves(jnp.exp(-rate * lanes_of(BLK).astype(F32))), axis=0)
    split = jnp.concatenate(halves(lags), axis=0)
    coef = jnp.zeros((STEP, BLK), F32)
    for o in range(SPAN + 1):
        both = mm(split[:, o * BLK : (o + 1) * BLK], fade, NT)
        term = both[:STEP, :BLK] + both[:STEP, BLK:] + both[STEP:, :BLK]
        coef = coef + term * jnp.exp(-row * float(o * BLK))
    cross = jnp.sum(cross_ref[0], axis=0, keepdims=True)
    coef = fold(jnp.where(own_group(STEP), (coef + cross) * root_ref[0, 0:1, :], 0.0))
    lag_ref[...] = jnp.concatenate((lags[:, : SPAN * BLK], coef), axis=1) * scale


def join_kernel(row_ref, root_ref, end_ref, after_ref, lag_ref, out_ref, *, scale):
    for step in range(row_ref.shape[0]):
        rows = slice(STEP * step, STEP * (step + 1))
        skip = jnp.exp(-row_ref[step, 0:1, :] * float(SPAN * BLK))
        cross = jnp.sum(end_ref[step] * after_ref[step], axis=0, keepdims=True)
        cross = cross * skip * root_ref[step, 0:1, :] * scale
        coef = fold(jnp.where(own_group(STEP), cross, 0.0))
        out_ref[rows, : SPAN * BLK] = lag_ref[rows, : SPAN * BLK]
        out_ref[rows, SPAN * BLK :] = lag_ref[rows, SPAN * BLK :] + coef


def main_kernel(
    q_ref, rate_ref, gain_ref, row_ref, table_ref, car_ref, ret_ref, before_ref, after_ref,
    p0, p1, p2, p3, xa, xb, ya, yb, o0, o1, o2, o3, xs, ys, fs, bs,
):
    q = q_ref[0]
    gather_blocks(q, (p0, p1, p2, p3), (xa, ya), (xb, yb), xs, ys)
    rate = rate_ref[...].reshape(BLK, BLK)
    gain = gain_ref[...].reshape(BLK, BLK)
    tok = lanes_of(BLK).astype(F32)
    row = row_ref[0, 0:1, :]
    same = own_group(BLK)
    shift = float(SPAN * BLK)
    out_f = (gain * jnp.exp(-rate * (tok + 1.0 + shift))).astype(BF16)
    out_b = (gain * jnp.exp(-rate * (BLK - 1.0 - tok + shift))).astype(BF16)
    out_f = jnp.concatenate((out_f, out_f), axis=0)
    out_b = jnp.concatenate((out_b, out_b), axis=0)

    def spread(ref):
        return jnp.where(same, jnp.concatenate([ref[0]] * STEP, axis=0), 0.0)

    start = spread(before_ref)
    stop = spread(after_ref)
    none = jnp.zeros((BLK, BLK), BF16)
    far_f, far_b = [], []
    for i in range(SPAN):
        left = none if i == 0 else car_ref[0, i - 1]
        rest = (start * jnp.exp(-row * float(BLK * i))).astype(BF16)
        far_f.append(mm(jnp.concatenate((left, rest), axis=1), out_f))
        left = none if i == SPAN - 1 else ret_ref[0, i]
        rest = (stop * jnp.exp(-row * float(BLK * (SPAN - 1 - i)))).astype(BF16)
        far_b.append(mm(jnp.concatenate((left, rest), axis=1), out_b))
    for i in range(SPAN):
        fs[i] = far_f[i]
        bs[i] = far_b[i]
    for g in range(STEP):
        rows = slice(GROUP * g, GROUP * (g + 1))
        x = [xs[j, rows, :] for j in range(2 * SPAN)]
        y = [ys[j, rows, :] for j in range(2 * SPAN)]
        wide_x = jnp.concatenate(
            [jnp.concatenate(x[SPAN - o : 2 * SPAN - o], axis=0) for o in range(SPAN + 1)], axis=1
        )
        wide_y = jnp.concatenate(
            [jnp.concatenate(y[o : o + SPAN], axis=0) for o in range(SPAN + 1)], axis=1
        )
        table = table_ref[g]
        tall = jnp.concatenate(
            [table[:, o * BLK : (o + 1) * BLK] for o in range(SPAN + 1)], axis=0
        )
        forward = mm(wide_x, tall)
        backward = mm(wide_y, table, NT)
        for i in range(SPAN):
            cut = slice(GROUP * i, GROUP * (i + 1))
            fs[i, rows, :] += forward[cut]
            bs[i, rows, :] += backward[cut]
    for m, out in enumerate((o0, o1, o2, o3)):
        out[0] = fs[q ^ m].astype(BF16)
        out[1] = bs[q ^ m].astype(BF16)


def sum_kernel(q_ref, s0, s1, s2, s3, med_ref, res_ref, turned):
    q = q_ref[0]
    local = s0.shape[0]
    for m, part in enumerate((s0, s1, s2, s3)):
        at = pl.ds(pl.multiple_of((q ^ m) * local, local), local)
        med_ref[at, :] = part[:, : SPAN * BLK]
        turned[at, :] = part[:, SPAN * BLK :]
    res_ref[...] = turned[...].T[:GROUP]


def gate_kernel(q_ref, *refs):
    q = q_ref[0]
    pieces, (go_ref, v_ref, k_ref, gq_ref, gk_ref, gv_ref) = refs[:-6], refs[-6:]
    part = pieces[0].shape[1]
    parts = len(pieces) // SPAN
    for h in range(parts):
        for m in range(SPAN):
            piece = pieces[h * SPAN + m]
            at = pl.ds(pl.multiple_of((q ^ m) * (part * parts) + h * part, part), part)
            gq_ref[at, :] = (go_ref[at, :].astype(F32) * piece[0].astype(F32)).astype(BF16)
            grad = piece[1].astype(F32)
            gk_ref[at, :] = (grad * v_ref[at, :].astype(F32)).astype(BF16)
            gv_ref[at, :] = (grad * k_ref[at, :].astype(F32)).astype(BF16)


def body(query, key_in, value_in, grad_out, med_filter, residues, pole_rate):
    channels, length = query.shape
    groups = channels // GROUP
    devices = lax.axis_size("ctx")
    seq_total = length * devices
    ranks = SPAN
    units = devices // ranks
    sub = channels // ranks
    local = groups // ranks
    index = lax.axis_index("ctx")
    q = lax.rem(index, ranks).astype(jnp.int32)
    q_arr = q.reshape(1)

    def swap(value, m):
        return lax.ppermute(value, "ctx", [(i, i ^ m) for i in range(devices)])

    def shift(value, by):
        by = by * ranks
        return lax.ppermute(
            value, "ctx", [(i, i + by) for i in range(devices) if 0 <= i + by < devices]
        )

    def part(m):
        def cut(array):
            return lax.dynamic_slice_in_dim(array, (q ^ m) * sub, sub, 0).astype(F32)

        return jnp.stack(
            [
                (cut(key_in) * cut(value_in)).astype(BF16),
                (cut(grad_out) * cut(query)).astype(BF16),
            ]
        )

    pieces = [part(0)] + [swap(part(m), m) for m in range(1, ranks)]

    x_near = shift(jnp.stack([pieces[0][0], pieces[1][0]]), 1)
    y_near = shift(jnp.stack([pieces[0][1], pieces[1][1]]), -1)
    x_far = shift(jnp.stack([pieces[2][0], pieces[3][0]]), 1)
    y_far = shift(jnp.stack([pieces[2][1], pieces[3][1]]), -1)

    rate = lax.dynamic_slice_in_dim(pole_rate, q * local, local, 1).T / seq_total
    res = lax.dynamic_slice_in_dim(residues, q * local, local, 1).T
    med = lax.dynamic_slice_in_dim(med_filter, q * local, local, 0)
    root = jnp.sqrt(-jnp.expm1(-2.0 * rate))
    rate_wide = jnp.broadcast_to(rate[:, :, None], (local, GROUP, BLK))
    gain_wide = jnp.broadcast_to((res * root)[:, :, None], (local, GROUP, BLK))

    steps = local // STEP
    rows = STEP * GROUP

    def flat(value):
        return jnp.broadcast_to(value.reshape(steps, 1, BLK), (steps, 8, BLK))

    rate_row = flat(rate)
    root_row = flat(root)
    scale = 1.0 / math.sqrt(GROUP * seq_total)
    params = pltpu.CompilerParams(vmem_limit_bytes=40 << 20)
    smem = pl.BlockSpec(memory_space=pltpu.SMEM)
    whole = pl.BlockSpec(memory_space=pltpu.VMEM)

    def block(shape, axis, offset=0):
        def at(i):
            return tuple(i + offset if d == axis else 0 for d in range(len(shape)))

        return pl.BlockSpec(shape, at)

    def specs(offset=0):
        return dict(
            group=block((STEP, GROUP, BLK), 0, offset),
            row=block((1, 8, BLK), 0, offset),
            packed=block((1, GROUP, BLK), 0, offset),
            pair=block((2, rows, BLK), 1, offset),
            states=block((1, SPAN - 1, BLK, BLK), 0, offset),
            table=block((STEP, BLK, WIDE), 0, offset),
            lag=block((STEP, WIDE), 0, offset),
        )

    sp = specs()
    table = pl.pallas_call(
        table_kernel,
        grid=(steps,),
        in_specs=[sp["group"], sp["group"], block((STEP, SPAN * BLK), 0)],
        out_specs=sp["table"],
        out_shape=jax.ShapeDtypeStruct((local, BLK, WIDE), BF16),
        compiler_params=params,
        name="tables",
    )(rate_wide, gain_wide, med)

    store = jax.ShapeDtypeStruct((steps, SPAN - 1, BLK, BLK), BF16)
    small = jax.ShapeDtypeStruct((steps, GROUP, BLK), F32)
    blocks = pltpu.VMEM((2 * SPAN, rows, BLK), BF16)
    halo = (x_near, x_far, y_near, y_far)
    carried, returned, ends, ahead, behind, cross = pl.pallas_call(
        state_kernel,
        grid=(steps,),
        in_specs=[smem, sp["group"], sp["row"]] + [sp["pair"]] * 8,
        out_specs=[sp["states"]] * 2 + [sp["packed"]] * 4,
        out_shape=[store] * 2 + [small] * 4,
        scratch_shapes=[blocks] * 2,
        compiler_params=params,
        name="states",
    )(q_arr, rate_wide, rate_row, *pieces, *halo)

    reach = 2
    while reach < units - 2:
        fade = jnp.exp(-rate_row[:, :1] * float(reach * ranks * length))
        ahead, behind = ahead + fade * shift(ahead, reach), behind + fade * shift(behind, -reach)
        reach *= 2
    before = shift(ahead, 2)
    after = shift(behind, -2)

    lag = pl.pallas_call(
        functools.partial(lag_kernel, scale=scale),
        grid=(steps,),
        in_specs=[smem, sp["group"], sp["row"], sp["row"], sp["packed"]] + [sp["pair"]] * 6,
        out_specs=sp["lag"],
        out_shape=jax.ShapeDtypeStruct((local, WIDE), F32),
        scratch_shapes=[pltpu.VMEM((SPAN, rows, BLK), BF16), blocks],
        compiler_params=params,
        name="lags",
    )(q_arr, rate_wide, rate_row, root_row, cross, *pieces, y_near, y_far)

    sums = pl.pallas_call(
        functools.partial(join_kernel, scale=scale),
        in_specs=[whole] * 5,
        out_specs=whole,
        out_shape=jax.ShapeDtypeStruct((local, WIDE), F32),
        compiler_params=params,
        name="joins",
    )(rate_row, root_row, ends, after, lag)

    back = []
    parts = PARTS
    for h in range(parts):
        sh = specs(h * (steps // parts))
        so = specs()
        outs = pl.pallas_call(
            main_kernel,
            grid=(steps // parts,),
            in_specs=[smem, sh["group"], sh["group"], sh["row"], sh["table"]]
            + [sh["states"]] * 2
            + [sh["packed"]] * 2
            + [sh["pair"]] * 8,
            out_specs=[so["pair"]] * 4,
            out_shape=[jax.ShapeDtypeStruct((2, sub // parts, BLK), BF16)] * 4,
            scratch_shapes=[blocks] * 2 + [pltpu.VMEM((SPAN, rows, BLK), F32)] * 2,
            compiler_params=params,
            name="convs",
        )(
            q_arr, rate_wide, gain_wide, rate_row, table, carried, returned, before, after,
            *pieces, *halo,
        )
        back += [outs[0]] + [swap(outs[m], m) for m in range(1, ranks)]

    hop = 1
    while hop < units:
        sums = sums + swap(sums, hop * ranks)
        hop *= 2
    parts_of = [sums] + [swap(sums, m) for m in range(1, ranks)]

    grads = pl.pallas_call(
        gate_kernel,
        in_specs=[smem] + [whole] * (len(back) + 3),
        out_specs=[whole] * 3,
        out_shape=[jax.ShapeDtypeStruct((channels, length), BF16)] * 3,
        compiler_params=params,
        name="gates",
    )(q_arr, *back, grad_out, value_in, key_in)
    grad_med, grad_res = pl.pallas_call(
        sum_kernel,
        in_specs=[smem] + [whole] * ranks,
        out_specs=[whole] * 2,
        out_shape=[
            jax.ShapeDtypeStruct((groups, SPAN * BLK), F32),
            jax.ShapeDtypeStruct((GROUP, groups), F32),
        ],
        scratch_shapes=[pltpu.VMEM((groups, BLK), F32)],
        compiler_params=params,
        name="sums",
    )(q_arr, *parts_of)
    return (*grads, grad_med, grad_res)


def solution(mesh):
    in_specs = (
        P("ch", "ctx"),
        P("ch", "ctx"),
        P("ch", "ctx"),
        P("ch", "ctx"),
        P("ch", None),
        P(None, "ch"),
        P(None, "ch"),
    )
    out_specs = (P("ch", "ctx"), P("ch", "ctx"), P("ch", "ctx"), P("ch", None), P(None, "ch"))
    return jax.shard_map(body, mesh=mesh, in_specs=in_specs, out_specs=out_specs, check_vma=False)
```

```python
import functools
import math

import jax
import jax.numpy as jnp
from jax import lax
from jax.experimental import pallas as pl
from jax.experimental.pallas import tpu as pltpu
from jax.sharding import PartitionSpec as P

GROUP = 16
BLK = 128
SPAN = 4
STEP = 8
PARTS = 2
WIDE = (SPAN + 1) * BLK
F32 = jnp.float32
BF16 = jnp.bfloat16
NT = (((1,), (1,)), ((), ()))
TN = (((0,), (0,)), ((), ()))
NN = (((1,), (0,)), ((), ()))


def mm(left, right, dims=NN):
    return lax.dot_general(left, right, dims, preferred_element_type=F32)


def halves(value):
    high = value.astype(BF16)
    return high, (value - high.astype(F32)).astype(BF16)


def lanes_of(rows):
    return lax.broadcasted_iota(jnp.int32, (rows, BLK), 1)


def table_kernel(row_ref, rate_ref, gain_ref, med_ref, table_ref, next_ref):
    next_ref[...] = row_ref[...]
    lane = lanes_of(GROUP).astype(F32)
    for g in range(STEP):
        rate = rate_ref[g]
        gain = gain_ref[g]
        pieces = [jnp.zeros((1, BLK), F32)]
        for o in range(SPAN + 1):
            tail = jnp.sum(gain * jnp.exp(-rate * (lane + float(o * BLK))), axis=0, keepdims=True)
            if o < SPAN:
                tail = tail + med_ref[g : g + 1, o * BLK : (o + 1) * BLK].astype(F32)
            pieces.append(tail)
        taps = jnp.broadcast_to(jnp.concatenate(pieces, axis=1), (GROUP, WIDE + BLK))
        skewed = pltpu.roll(taps, 0, 1, stride=1, stride_axis=0)
        for i in range(BLK // GROUP):
            moved = skewed if i == 0 else pltpu.roll(skewed, GROUP * i, 1)
            table_ref[g, GROUP * i : GROUP * (i + 1), :] = moved[:, BLK:].astype(BF16)


def own_group(rows):
    row = lax.broadcasted_iota(jnp.int32, (rows, BLK), 0) // (rows // STEP)
    return row == lax.broadcasted_iota(jnp.int32, (rows, BLK), 1) // GROUP


def column_sum(value):
    total = value[0:GROUP]
    for g in range(1, STEP):
        total = total + value[GROUP * g : GROUP * (g + 1)]
    return total


def gather_blocks(q, pieces, near, far, xs, ys):
    for m, piece in enumerate(pieces):
        xs[SPAN + (q ^ m)] = piece[0]
        ys[q ^ m] = piece[1]
    for m in range(SPAN):
        x_part, y_part = near if m < 2 else far
        xs[q ^ m] = x_part[m % 2]
        ys[SPAN + (q ^ m)] = y_part[m % 2]


def state_kernel(
    q_ref, rate_ref, row_ref, p0, p1, p2, p3, xa, xb, ya, yb,
    car_ref, ret_ref, end_ref, ahead_ref, behind_ref, mail_ref, cross_ref, xs, ys,
):
    gather_blocks(q_ref[0] & 3, (p0, p1, p2, p3), (xa, ya), (xb, yb), xs, ys)
    rate = rate_ref[...].reshape(BLK, BLK)
    tok = lanes_of(BLK).astype(F32)
    row = row_ref[0, 0:1, :]
    decay = jnp.exp(-row * float(BLK))
    skip = jnp.exp(-row * float(SPAN * BLK))
    same = own_group(BLK)
    fin = jnp.concatenate(halves(jnp.exp(-rate * (BLK - 1.0 - tok))), axis=0)
    ini = jnp.concatenate(halves(jnp.exp(-rate * (tok + 1.0))), axis=0)

    def state(blocks, j, weights):
        both = mm(blocks[j], weights, NT)
        return jnp.where(same, both[:, :BLK] + both[:, BLK:], 0.0)

    carried = state(xs, 0, fin)
    for i in range(1, SPAN):
        car_ref[0, i - 1] = carried.astype(BF16)
        carried = carried * decay + state(xs, i, fin)
    own = [state(xs, SPAN + i, fin) for i in range(SPAN)]
    end = own[0]
    for i in range(1, SPAN):
        end = end * decay + own[i]
    end_ref[0] = column_sum(end)
    ahead = column_sum(end + skip * carried)
    ahead_ref[0] = ahead

    returned = state(ys, 2 * SPAN - 1, ini)
    cross = jnp.zeros((BLK, BLK), F32)
    for i in range(SPAN - 2, -1, -1):
        ret_ref[0, i] = returned.astype(BF16)
        cross = cross + own[i] * returned
        returned = returned * decay + state(ys, SPAN + i, ini)
    head = state(ys, SPAN - 1, ini)
    for i in range(SPAN - 2, -1, -1):
        head = head * decay + state(ys, i, ini)
    behind = column_sum(head + skip * returned)
    behind_ref[0] = behind
    mail_ref[0] = jnp.where((q_ref[0] & 4) > 0, ahead, behind)
    cross_ref[0] = column_sum(cross) * skip


def roll_left(value, amount):
    width = value.shape[1]
    return value if amount % width == 0 else pltpu.roll(value, width - amount, 1)


def fold(value):
    for step in (64, 32, 16):
        value = value + pltpu.roll(value, step, 1)
    return value


def lag_kernel(
    q_ref, rate_ref, row_ref, root_ref, cross_ref, p0, p1, p2, p3, ya, yb, lag_ref, xs, ys, sums,
    *, scale,
):
    q = q_ref[0] & 3
    for m, piece in enumerate((p0, p1, p2, p3)):
        xs[q ^ m] = piece[0]
        ys[q ^ m] = piece[1]
        ys[SPAN + (q ^ m)] = (ya if m < 2 else yb)[m % 2]
    row_at = lax.broadcasted_iota(jnp.int32, (BLK, BLK), 0)
    causal = lanes_of(BLK) >= row_at
    lane8 = lanes_of(8)
    for g in range(STEP):
        rows = slice(GROUP * g, GROUP * (g + 1))
        y = [ys[j, rows, :] for j in range(2 * SPAN)]
        wide_y = jnp.concatenate(
            [jnp.concatenate(y[o : o + SPAN], axis=0) for o in range(SPAN + 1)], axis=1
        )
        own_x = jnp.concatenate([xs[j, rows, :] for j in range(SPAN)], axis=0)
        pairs = mm(own_x, wide_y, TN)
        tiles = [pairs[:, o * BLK : (o + 1) * BLK] for o in range(SPAN + 1)]
        tiles[0] = jnp.where(causal, tiles[0], 0.0)
        count = BLK // 8
        parts = [[tile[8 * i : 8 * (i + 1)] for i in range(count)] for tile in tiles]
        while count > 1:
            count //= 2
            keep = lane8 < BLK - 8 * count
            moved = [
                [pltpu.roll(part[i + count], BLK - 8 * count, 1) for i in range(count)]
                for part in parts
            ]
            for o in range(SPAN + 1):
                for i in range(count):
                    after = moved[o + 1][i] if o < SPAN else 0.0
                    parts[o][i] = parts[o][i] + jnp.where(keep, moved[o][i], after)
        for o in range(SPAN + 1):
            sums[g, :, o * BLK : (o + 1) * BLK] = parts[o][0]
    lags = sums[:, 0, :]
    for r in range(1, 8):
        lags = lags + roll_left(sums[:, r, :], r)
    rate = rate_ref[...].reshape(BLK, BLK)
    row = row_ref[0, 0:1, :]
    fade = jnp.concatenate(halves(jnp.exp(-rate * lanes_of(BLK).astype(F32))), axis=0)
    split = jnp.concatenate(halves(lags), axis=0)
    coef = jnp.zeros((STEP, BLK), F32)
    for o in range(SPAN + 1):
        both = mm(split[:, o * BLK : (o + 1) * BLK], fade, NT)
        term = both[:STEP, :BLK] + both[:STEP, BLK:] + both[STEP:, :BLK]
        coef = coef + term * jnp.exp(-row * float(o * BLK))
    cross = jnp.sum(cross_ref[0], axis=0, keepdims=True)
    coef = fold(jnp.where(own_group(STEP), (coef + cross) * root_ref[0, 0:1, :], 0.0))
    lag_ref[...] = jnp.concatenate((lags[:, : SPAN * BLK], coef), axis=1) * scale


def join_kernel(q_ref, row_ref, root_ref, end_ref, after_ref, lag_ref, out_ref, *, scale):
    for step in range(row_ref.shape[0]):
        rows = slice(STEP * step, STEP * (step + 1))
        skip = jnp.exp(-row_ref[step, 0:1, :] * float(SPAN * BLK))
        cross = jnp.sum(end_ref[step] * after_ref[step], axis=0, keepdims=True)
        cross = cross * skip * root_ref[step, 0:1, :] * scale
        coef = fold(jnp.where(own_group(STEP) & ((q_ref[0] & 16) > 0), cross, 0.0))
        out_ref[rows, : SPAN * BLK] = lag_ref[rows, : SPAN * BLK]
        out_ref[rows, SPAN * BLK :] = lag_ref[rows, SPAN * BLK :] + coef


def main_kernel(
    q_ref, rate_ref, gain_ref, row_ref, table_ref, car_ref, ret_ref, before_ref, after_ref,
    p0, p1, p2, p3, xa, xb, ya, yb, o0, o1, o2, o3, xs, ys, fs, bs,
):
    q = q_ref[0] & 3
    gather_blocks(q, (p0, p1, p2, p3), (xa, ya), (xb, yb), xs, ys)
    rate = rate_ref[...].reshape(BLK, BLK)
    gain = gain_ref[...].reshape(BLK, BLK)
    tok = lanes_of(BLK).astype(F32)
    row = row_ref[0, 0:1, :]
    same = own_group(BLK)
    shift = float(SPAN * BLK)
    out_f = (gain * jnp.exp(-rate * (tok + 1.0 + shift))).astype(BF16)
    out_b = (gain * jnp.exp(-rate * (BLK - 1.0 - tok + shift))).astype(BF16)
    out_f = jnp.concatenate((out_f, out_f), axis=0)
    out_b = jnp.concatenate((out_b, out_b), axis=0)

    def spread(ref, flag):
        return jnp.where(same & (flag > 0), jnp.concatenate([ref[0]] * STEP, axis=0), 0.0)

    start = spread(before_ref, q_ref[0] & 8)
    stop = spread(after_ref, q_ref[0] & 16)
    none = jnp.zeros((BLK, BLK), BF16)
    far_f, far_b = [], []
    for i in range(SPAN):
        left = none if i == 0 else car_ref[0, i - 1]
        rest = (start * jnp.exp(-row * float(BLK * i))).astype(BF16)
        far_f.append(mm(jnp.concatenate((left, rest), axis=1), out_f))
        left = none if i == SPAN - 1 else ret_ref[0, i]
        rest = (stop * jnp.exp(-row * float(BLK * (SPAN - 1 - i)))).astype(BF16)
        far_b.append(mm(jnp.concatenate((left, rest), axis=1), out_b))
    for i in range(SPAN):
        fs[i] = far_f[i]
        bs[i] = far_b[i]
    for g in range(STEP):
        rows = slice(GROUP * g, GROUP * (g + 1))
        x = [xs[j, rows, :] for j in range(2 * SPAN)]
        y = [ys[j, rows, :] for j in range(2 * SPAN)]
        wide_x = jnp.concatenate(
            [jnp.concatenate(x[SPAN - o : 2 * SPAN - o], axis=0) for o in range(SPAN + 1)], axis=1
        )
        wide_y = jnp.concatenate(
            [jnp.concatenate(y[o : o + SPAN], axis=0) for o in range(SPAN + 1)], axis=1
        )
        table = table_ref[g]
        tall = jnp.concatenate(
            [table[:, o * BLK : (o + 1) * BLK] for o in range(SPAN + 1)], axis=0
        )
        forward = mm(wide_x, tall)
        backward = mm(wide_y, table, NT)
        for i in range(SPAN):
            cut = slice(GROUP * i, GROUP * (i + 1))
            fs[i, rows, :] += forward[cut]
            bs[i, rows, :] += backward[cut]
    for m, out in enumerate((o0, o1, o2, o3)):
        out[0] = fs[q ^ m].astype(BF16)
        out[1] = bs[q ^ m].astype(BF16)


def sum_kernel(q_ref, s0, s1, s2, s3, med_ref, res_ref, turned):
    q = q_ref[0] & 3
    local = s0.shape[0]
    for m, part in enumerate((s0, s1, s2, s3)):
        at = pl.ds(pl.multiple_of((q ^ m) * local, local), local)
        med_ref[at, :] = part[:, : SPAN * BLK]
        turned[at, :] = part[:, SPAN * BLK :]
    res_ref[...] = turned[...].T[:GROUP]


def gate_kernel(q_ref, *refs):
    q = q_ref[0] & 3
    pieces, (go_ref, v_ref, k_ref, gq_ref, gk_ref, gv_ref) = refs[:-6], refs[-6:]
    part = pieces[0].shape[1]
    parts = len(pieces) // SPAN
    for h in range(parts):
        for m in range(SPAN):
            piece = pieces[h * SPAN + m]
            at = pl.ds(pl.multiple_of((q ^ m) * (part * parts) + h * part, part), part)
            gq_ref[at, :] = (go_ref[at, :].astype(F32) * piece[0].astype(F32)).astype(BF16)
            grad = piece[1].astype(F32)
            gk_ref[at, :] = (grad * v_ref[at, :].astype(F32)).astype(BF16)
            gv_ref[at, :] = (grad * k_ref[at, :].astype(F32)).astype(BF16)


def body(query, key_in, value_in, grad_out, med_filter, residues, pole_rate):
    channels, length = query.shape
    groups = channels // GROUP
    devices = lax.axis_size("ctx")
    seq_total = length * devices
    ranks = SPAN
    units = devices // ranks
    sub = channels // ranks
    local = groups // ranks
    index = lax.axis_index("ctx")
    q = lax.rem(index, ranks).astype(jnp.int32)
    low = (index < 2 * ranks).astype(jnp.int32)
    one = jnp.int32(1)
    ahead_on, behind_on = (one - low, low) if units == 4 else (one, one)
    q_arr = (q + 4 * low + 8 * ahead_on + 16 * behind_on).reshape(1)

    def swap(value, m):
        return lax.ppermute(value, "ctx", [(i, i ^ m) for i in range(devices)])

    def shift(value, by):
        by = by * ranks
        return lax.ppermute(
            value, "ctx", [(i, i + by) for i in range(devices) if 0 <= i + by < devices]
        )

    def part(m):
        def cut(array):
            return lax.dynamic_slice_in_dim(array, (q ^ m) * sub, sub, 0).astype(F32)

        return jnp.stack(
            [
                (cut(key_in) * cut(value_in)).astype(BF16),
                (cut(grad_out) * cut(query)).astype(BF16),
            ]
        )

    pieces = [part(0)] + [swap(part(m), m) for m in range(1, ranks)]

    x_near = shift(jnp.stack([pieces[0][0], pieces[1][0]]), 1)
    y_near = shift(jnp.stack([pieces[0][1], pieces[1][1]]), -1)
    rate = lax.dynamic_slice_in_dim(pole_rate, q * local, local, 1).T / seq_total
    res = lax.dynamic_slice_in_dim(residues, q * local, local, 1).T
    med = lax.dynamic_slice_in_dim(med_filter, q * local, local, 0)
    root = jnp.sqrt(-jnp.expm1(-2.0 * rate))
    rate_wide = jnp.broadcast_to(rate[:, :, None], (local, GROUP, BLK))
    gain_wide = jnp.broadcast_to((res * root)[:, :, None], (local, GROUP, BLK))

    steps = local // STEP
    rows = STEP * GROUP

    def flat(value):
        return jnp.broadcast_to(value.reshape(steps, 1, BLK), (steps, 8, BLK))

    rate_row = flat(rate)
    root_row = flat(root)
    scale = 1.0 / math.sqrt(GROUP * seq_total)
    params = pltpu.CompilerParams(vmem_limit_bytes=8 << 20)
    smem = pl.BlockSpec(memory_space=pltpu.SMEM)
    whole = pl.BlockSpec(memory_space=pltpu.VMEM)

    def block(shape, axis, offset=0):
        def at(i):
            return tuple(i + offset if d == axis else 0 for d in range(len(shape)))

        return pl.BlockSpec(shape, at)

    def specs(offset=0):
        return dict(
            group=block((STEP, GROUP, BLK), 0, offset),
            row=block((1, 8, BLK), 0, offset),
            packed=block((1, GROUP, BLK), 0, offset),
            pair=block((2, rows, BLK), 1, offset),
            states=block((1, SPAN - 1, BLK, BLK), 0, offset),
            table=block((STEP, BLK, WIDE), 0, offset),
            lag=block((STEP, WIDE), 0, offset),
        )

    sp = specs()
    pieces[2], pieces[3], x_near, y_near, rate_row, root_row = lax.optimization_barrier(
        (pieces[2], pieces[3], x_near, y_near, rate_row, root_row)
    )
    x_far = shift(jnp.stack([pieces[2][0], pieces[3][0]]), 1)
    y_far = shift(jnp.stack([pieces[2][1], pieces[3][1]]), -1)

    table, rate_row = pl.pallas_call(
        table_kernel,
        grid=(steps,),
        in_specs=[sp["row"], sp["group"], sp["group"], block((STEP, SPAN * BLK), 0)],
        out_specs=[sp["table"], sp["row"]],
        out_shape=[
            jax.ShapeDtypeStruct((local, BLK, WIDE), BF16),
            jax.ShapeDtypeStruct(rate_row.shape, F32),
        ],
        compiler_params=params,
        name="tables",
    )(rate_row, rate_wide, gain_wide, med)

    store = jax.ShapeDtypeStruct((steps, SPAN - 1, BLK, BLK), BF16)
    small = jax.ShapeDtypeStruct((steps, GROUP, BLK), F32)
    blocks = pltpu.VMEM((2 * SPAN, rows, BLK), BF16)
    halo = (x_near, x_far, y_near, y_far)
    carried, returned, ends, ahead, behind, mail, cross = pl.pallas_call(
        state_kernel,
        grid=(steps,),
        in_specs=[smem, sp["group"], sp["row"]] + [sp["pair"]] * 8,
        out_specs=[sp["states"]] * 2 + [sp["packed"]] * 5,
        out_shape=[store] * 2 + [small] * 5,
        scratch_shapes=[blocks] * 2,
        compiler_params=params,
        name="states",
    )(q_arr, rate_wide, rate_row, *pieces, *halo)

    if units == 4:
        before = after = swap(mail, 2 * ranks)
    else:
        reach = 2
        while reach < units - 2:
            fade = jnp.exp(-rate_row[:, :1] * float(reach * ranks * length))
            ahead, behind = (
                ahead + fade * shift(ahead, reach),
                behind + fade * shift(behind, -reach),
            )
            reach *= 2
        before = shift(ahead, 2)
        after = shift(behind, -2)

    lag = pl.pallas_call(
        functools.partial(lag_kernel, scale=scale),
        grid=(steps,),
        in_specs=[smem, sp["group"], sp["row"], sp["row"], sp["packed"]] + [sp["pair"]] * 6,
        out_specs=sp["lag"],
        out_shape=jax.ShapeDtypeStruct((local, WIDE), F32),
        scratch_shapes=[
            pltpu.VMEM((SPAN, rows, BLK), BF16),
            blocks,
            pltpu.VMEM((STEP, 8, WIDE), F32),
        ],
        compiler_params=params,
        name="lags",
    )(q_arr, rate_wide, rate_row, root_row, cross, *pieces, y_near, y_far)
    before, after, lag = lax.optimization_barrier((before, after, lag))

    sums = pl.pallas_call(
        functools.partial(join_kernel, scale=scale),
        in_specs=[smem] + [whole] * 5,
        out_specs=whole,
        out_shape=jax.ShapeDtypeStruct((local, WIDE), F32),
        compiler_params=params,
        name="joins",
    )(q_arr, rate_row, root_row, ends, after, lag)

    back = []
    parts = PARTS
    q_next = q_arr
    for h in range(parts):
        sh = specs(h * (steps // parts))
        so = specs()
        outs = pl.pallas_call(
            main_kernel,
            grid=(steps // parts,),
            in_specs=[smem, sh["group"], sh["group"], sh["row"], sh["table"]]
            + [sh["states"]] * 2
            + [sh["packed"]] * 2
            + [sh["pair"]] * 8,
            out_specs=[so["pair"]] * 4,
            out_shape=[jax.ShapeDtypeStruct((2, sub // parts, BLK), BF16)] * 4,
            scratch_shapes=[blocks] * 2 + [pltpu.VMEM((SPAN, rows, BLK), F32)] * 2,
            compiler_params=params,
            name="convs",
        )(
            q_next, rate_wide, gain_wide, rate_row, table, carried, returned, before, after,
            *pieces, *halo,
        )
        outs = list(outs)
        outs[0], q_next = lax.optimization_barrier((outs[0], q_arr))
        back += [outs[0]] + [swap(outs[m], m) for m in range(1, ranks)]

    hop = 1
    while hop < units:
        if hop == 2:
            back[2], back[3], sums = lax.optimization_barrier((back[2], back[3], sums))
        sums = sums + swap(sums, hop * ranks)
        hop *= 2
    parts_of = [sums] + [swap(sums, m) for m in range(1, ranks)]

    grads = pl.pallas_call(
        gate_kernel,
        in_specs=[smem] + [whole] * (len(back) + 3),
        out_specs=[whole] * 3,
        out_shape=[jax.ShapeDtypeStruct((channels, length), BF16)] * 3,
        compiler_params=params,
        name="gates",
    )(q_arr, *back, grad_out, value_in, key_in)
    grad_med, grad_res = pl.pallas_call(
        sum_kernel,
        in_specs=[smem] + [whole] * ranks,
        out_specs=[whole] * 2,
        out_shape=[
            jax.ShapeDtypeStruct((groups, SPAN * BLK), F32),
            jax.ShapeDtypeStruct((GROUP, groups), F32),
        ],
        scratch_shapes=[pltpu.VMEM((groups, BLK), F32)],
        compiler_params=params,
        name="sums",
    )(q_arr, *parts_of)
    return (*grads, grad_med, grad_res)


def solution(mesh):
    in_specs = (
        P("ch", "ctx"),
        P("ch", "ctx"),
        P("ch", "ctx"),
        P("ch", "ctx"),
        P("ch", None),
        P(None, "ch"),
        P(None, "ch"),
    )
    out_specs = (P("ch", "ctx"), P("ch", "ctx"), P("ch", "ctx"), P("ch", None), P(None, "ch"))
    return jax.shard_map(body, mesh=mesh, in_specs=in_specs, out_specs=out_specs, check_vma=False)
```

```python
import functools
import math

import jax
import jax.numpy as jnp
from jax import lax
from jax.experimental import pallas as pl
from jax.experimental.pallas import tpu as pltpu
from jax.sharding import PartitionSpec as P

GROUP = 16
BLK = 128
SPAN = 4
STEP = 8
PARTS = 2
WIDE = (SPAN + 1) * BLK
F32 = jnp.float32
BF16 = jnp.bfloat16
NT = (((1,), (1,)), ((), ()))
TN = (((0,), (0,)), ((), ()))
NN = (((1,), (0,)), ((), ()))


def mm(left, right, dims=NN):
    return lax.dot_general(left, right, dims, preferred_element_type=F32)


def halves(value):
    high = value.astype(BF16)
    return high, (value - high.astype(F32)).astype(BF16)


def lanes_of(rows):
    return lax.broadcasted_iota(jnp.int32, (rows, BLK), 1)


def table_kernel(row_ref, rate_ref, gain_ref, med_ref, table_ref, next_ref):
    next_ref[...] = row_ref[...]
    lane = lanes_of(GROUP).astype(F32)
    for g in range(STEP):
        rate = rate_ref[g]
        gain = gain_ref[g]
        pieces = [jnp.zeros((1, BLK), F32)]
        for o in range(SPAN + 1):
            tail = jnp.sum(gain * jnp.exp(-rate * (lane + float(o * BLK))), axis=0, keepdims=True)
            if o < SPAN:
                tail = tail + med_ref[g : g + 1, o * BLK : (o + 1) * BLK].astype(F32)
            pieces.append(tail)
        taps = jnp.broadcast_to(jnp.concatenate(pieces, axis=1), (GROUP, WIDE + BLK))
        skewed = pltpu.roll(taps, 0, 1, stride=1, stride_axis=0)
        for i in range(BLK // GROUP):
            moved = skewed if i == 0 else pltpu.roll(skewed, GROUP * i, 1)
            table_ref[g, GROUP * i : GROUP * (i + 1), :] = moved[:, BLK:].astype(BF16)


def own_group(rows):
    row = lax.broadcasted_iota(jnp.int32, (rows, BLK), 0) // (rows // STEP)
    return row == lax.broadcasted_iota(jnp.int32, (rows, BLK), 1) // GROUP


def column_sum(value):
    total = value[0:GROUP]
    for g in range(1, STEP):
        total = total + value[GROUP * g : GROUP * (g + 1)]
    return total


def gather_blocks(q, pieces, near, far, xs, ys):
    for m, piece in enumerate(pieces):
        xs[SPAN + (q ^ m)] = piece[0]
        ys[q ^ m] = piece[1]
    for m in range(SPAN):
        x_part, y_part = near if m < 2 else far
        xs[q ^ m] = x_part[m % 2]
        ys[SPAN + (q ^ m)] = y_part[m % 2]


def state_kernel(
    q_ref, rate_ref, row_ref, p0, p1, p2, p3, xa, xb, ya, yb,
    car_ref, ret_ref, end_ref, ahead_ref, behind_ref, mail_ref, cross_ref, xs, ys,
):
    gather_blocks(q_ref[0] & 3, (p0, p1, p2, p3), (xa, ya), (xb, yb), xs, ys)
    rate = rate_ref[...].reshape(BLK, BLK)
    tok = lanes_of(BLK).astype(F32)
    row = row_ref[0, 0:1, :]
    decay = jnp.exp(-row * float(BLK))
    skip = jnp.exp(-row * float(SPAN * BLK))
    same = own_group(BLK)
    fin = jnp.concatenate(halves(jnp.exp(-rate * (BLK - 1.0 - tok))), axis=0)
    ini = jnp.concatenate(halves(jnp.exp(-rate * (tok + 1.0))), axis=0)

    def state(blocks, j, weights):
        both = mm(blocks[j], weights, NT)
        return jnp.where(same, both[:, :BLK] + both[:, BLK:], 0.0)

    carried = state(xs, 0, fin)
    for i in range(1, SPAN):
        car_ref[0, i - 1] = carried.astype(BF16)
        carried = carried * decay + state(xs, i, fin)
    own = [state(xs, SPAN + i, fin) for i in range(SPAN)]
    end = own[0]
    for i in range(1, SPAN):
        end = end * decay + own[i]
    end_ref[0] = column_sum(end)
    ahead = column_sum(end + skip * carried)
    ahead_ref[0] = ahead

    returned = state(ys, 2 * SPAN - 1, ini)
    cross = jnp.zeros((BLK, BLK), F32)
    for i in range(SPAN - 2, -1, -1):
        ret_ref[0, i] = returned.astype(BF16)
        cross = cross + own[i] * returned
        returned = returned * decay + state(ys, SPAN + i, ini)
    head = state(ys, SPAN - 1, ini)
    for i in range(SPAN - 2, -1, -1):
        head = head * decay + state(ys, i, ini)
    behind = column_sum(head + skip * returned)
    behind_ref[0] = behind
    mail_ref[0] = jnp.where((q_ref[0] & 4) > 0, ahead, behind)
    cross_ref[0] = column_sum(cross) * skip


def roll_left(value, amount):
    width = value.shape[1]
    return value if amount % width == 0 else pltpu.roll(value, width - amount, 1)


def fold(value):
    for step in (64, 32, 16):
        value = value + pltpu.roll(value, step, 1)
    return value


def lag_kernel(
    q_ref, rate_ref, row_ref, root_ref, cross_ref, p0, p1, p2, p3, ya, yb, lag_ref, xs, ys, sums,
    *, scale,
):
    q = q_ref[0] & 3
    for m, piece in enumerate((p0, p1, p2, p3)):
        xs[q ^ m] = piece[0]
        ys[q ^ m] = piece[1]
        ys[SPAN + (q ^ m)] = (ya if m < 2 else yb)[m % 2]
    row_at = lax.broadcasted_iota(jnp.int32, (BLK, BLK), 0)
    causal = lanes_of(BLK) >= row_at
    lane8 = lanes_of(8)
    for g in range(STEP):
        rows = slice(GROUP * g, GROUP * (g + 1))
        y = [ys[j, rows, :] for j in range(2 * SPAN)]
        wide_y = jnp.concatenate(
            [jnp.concatenate(y[o : o + SPAN], axis=0) for o in range(SPAN + 1)], axis=1
        )
        own_x = jnp.concatenate([xs[j, rows, :] for j in range(SPAN)], axis=0)
        pairs = mm(own_x, wide_y, TN)
        tiles = [pairs[:, o * BLK : (o + 1) * BLK] for o in range(SPAN + 1)]
        tiles[0] = jnp.where(causal, tiles[0], 0.0)
        count = BLK // 8
        parts = [[tile[8 * i : 8 * (i + 1)] for i in range(count)] for tile in tiles]
        while count > 1:
            count //= 2
            keep = lane8 < BLK - 8 * count
            moved = [
                [pltpu.roll(part[i + count], BLK - 8 * count, 1) for i in range(count)]
                for part in parts
            ]
            for o in range(SPAN + 1):
                for i in range(count):
                    after = moved[o + 1][i] if o < SPAN else 0.0
                    parts[o][i] = parts[o][i] + jnp.where(keep, moved[o][i], after)
        for o in range(SPAN + 1):
            sums[g, :, o * BLK : (o + 1) * BLK] = parts[o][0]
    lags = sums[:, 0, :]
    for r in range(1, 8):
        lags = lags + roll_left(sums[:, r, :], r)
    rate = rate_ref[...].reshape(BLK, BLK)
    row = row_ref[0, 0:1, :]
    fade = jnp.concatenate(halves(jnp.exp(-rate * lanes_of(BLK).astype(F32))), axis=0)
    split = jnp.concatenate(halves(lags), axis=0)
    coef = jnp.zeros((STEP, BLK), F32)
    for o in range(SPAN + 1):
        both = mm(split[:, o * BLK : (o + 1) * BLK], fade, NT)
        term = both[:STEP, :BLK] + both[:STEP, BLK:] + both[STEP:, :BLK]
        coef = coef + term * jnp.exp(-row * float(o * BLK))
    cross = jnp.sum(cross_ref[0], axis=0, keepdims=True)
    coef = fold(jnp.where(own_group(STEP), (coef + cross) * root_ref[0, 0:1, :], 0.0))
    lag_ref[...] = jnp.concatenate((lags[:, : SPAN * BLK], coef), axis=1) * scale


def join_kernel(q_ref, row_ref, root_ref, end_ref, after_ref, lag_ref, out_ref, *, scale):
    for step in range(row_ref.shape[0]):
        rows = slice(STEP * step, STEP * (step + 1))
        skip = jnp.exp(-row_ref[step, 0:1, :] * float(SPAN * BLK))
        cross = jnp.sum(end_ref[step] * after_ref[step], axis=0, keepdims=True)
        cross = cross * skip * root_ref[step, 0:1, :] * scale
        coef = fold(jnp.where(own_group(STEP) & ((q_ref[0] & 16) > 0), cross, 0.0))
        out_ref[rows, : SPAN * BLK] = lag_ref[rows, : SPAN * BLK]
        out_ref[rows, SPAN * BLK :] = lag_ref[rows, SPAN * BLK :] + coef


def main_kernel(
    q_ref, rate_ref, gain_ref, row_ref, table_ref, car_ref, ret_ref, before_ref, after_ref,
    p0, p1, p2, p3, xa, xb, ya, yb, o0, o1, o2, o3, xs, ys, fs, bs,
):
    q = q_ref[0] & 3
    gather_blocks(q, (p0, p1, p2, p3), (xa, ya), (xb, yb), xs, ys)
    rate = rate_ref[...].reshape(BLK, BLK)
    gain = gain_ref[...].reshape(BLK, BLK)
    tok = lanes_of(BLK).astype(F32)
    row = row_ref[0, 0:1, :]
    same = own_group(BLK)
    shift = float(SPAN * BLK)
    out_f = (gain * jnp.exp(-rate * (tok + 1.0 + shift))).astype(BF16)
    out_b = (gain * jnp.exp(-rate * (BLK - 1.0 - tok + shift))).astype(BF16)
    out_f = jnp.concatenate((out_f, out_f), axis=0)
    out_b = jnp.concatenate((out_b, out_b), axis=0)

    def spread(ref, flag):
        return jnp.where(same & (flag > 0), jnp.concatenate([ref[0]] * STEP, axis=0), 0.0)

    start = spread(before_ref, q_ref[0] & 8)
    stop = spread(after_ref, q_ref[0] & 16)
    none = jnp.zeros((BLK, BLK), BF16)
    far_f, far_b = [], []
    for i in range(SPAN):
        left = none if i == 0 else car_ref[0, i - 1]
        rest = (start * jnp.exp(-row * float(BLK * i))).astype(BF16)
        far_f.append(mm(jnp.concatenate((left, rest), axis=1), out_f))
        left = none if i == SPAN - 1 else ret_ref[0, i]
        rest = (stop * jnp.exp(-row * float(BLK * (SPAN - 1 - i)))).astype(BF16)
        far_b.append(mm(jnp.concatenate((left, rest), axis=1), out_b))
    for i in range(SPAN):
        fs[i] = far_f[i]
        bs[i] = far_b[i]
    for g in range(STEP):
        rows = slice(GROUP * g, GROUP * (g + 1))
        x = [xs[j, rows, :] for j in range(2 * SPAN)]
        y = [ys[j, rows, :] for j in range(2 * SPAN)]
        wide_x = jnp.concatenate(
            [jnp.concatenate(x[SPAN - o : 2 * SPAN - o], axis=0) for o in range(SPAN + 1)], axis=1
        )
        wide_y = jnp.concatenate(
            [jnp.concatenate(y[o : o + SPAN], axis=0) for o in range(SPAN + 1)], axis=1
        )
        table = table_ref[g]
        tall = jnp.concatenate(
            [table[:, o * BLK : (o + 1) * BLK] for o in range(SPAN + 1)], axis=0
        )
        forward = mm(wide_x, tall)
        backward = mm(wide_y, table, NT)
        for i in range(SPAN):
            cut = slice(GROUP * i, GROUP * (i + 1))
            fs[i, rows, :] += forward[cut]
            bs[i, rows, :] += backward[cut]
    for m, out in enumerate((o0, o1, o2, o3)):
        out[0] = fs[q ^ m].astype(BF16)
        out[1] = bs[q ^ m].astype(BF16)


def sum_kernel(q_ref, s0, s1, s2, s3, med_ref, res_ref, turned):
    q = q_ref[0] & 3
    local = s0.shape[0]
    for m, part in enumerate((s0, s1, s2, s3)):
        at = pl.ds(pl.multiple_of((q ^ m) * local, local), local)
        med_ref[at, :] = part[:, : SPAN * BLK].astype(F32)
        turned[at, :] = part[:, SPAN * BLK :].astype(F32)
    res_ref[...] = turned[...].T[:GROUP]


def gate_kernel(q_ref, *refs):
    q = q_ref[0] & 3
    pieces, (go_ref, v_ref, k_ref, gq_ref, gk_ref, gv_ref) = refs[:-6], refs[-6:]
    part = pieces[0].shape[1]
    parts = len(pieces) // SPAN
    for h in range(parts):
        for m in range(SPAN):
            piece = pieces[h * SPAN + m]
            at = pl.ds(pl.multiple_of((q ^ m) * (part * parts) + h * part, part), part)
            gq_ref[at, :] = (go_ref[at, :].astype(F32) * piece[0].astype(F32)).astype(BF16)
            grad = piece[1].astype(F32)
            gk_ref[at, :] = (grad * v_ref[at, :].astype(F32)).astype(BF16)
            gv_ref[at, :] = (grad * k_ref[at, :].astype(F32)).astype(BF16)


def body(query, key_in, value_in, grad_out, med_filter, residues, pole_rate):
    channels, length = query.shape
    groups = channels // GROUP
    devices = lax.axis_size("ctx")
    seq_total = length * devices
    ranks = SPAN
    units = devices // ranks
    sub = channels // ranks
    local = groups // ranks
    index = lax.axis_index("ctx")
    q = lax.rem(index, ranks).astype(jnp.int32)
    low = (index < 2 * ranks).astype(jnp.int32)
    one = jnp.int32(1)
    ahead_on, behind_on = (one - low, low) if units == 4 else (one, one)
    q_arr = (q + 4 * low + 8 * ahead_on + 16 * behind_on).reshape(1)

    def swap(value, m):
        return lax.ppermute(value, "ctx", [(i, i ^ m) for i in range(devices)])

    def shift(value, by):
        by = by * ranks
        return lax.ppermute(
            value, "ctx", [(i, i + by) for i in range(devices) if 0 <= i + by < devices]
        )

    def part(m):
        def cut(array):
            return lax.dynamic_slice_in_dim(array, (q ^ m) * sub, sub, 0).astype(F32)

        return jnp.stack(
            [
                (cut(key_in) * cut(value_in)).astype(BF16),
                (cut(grad_out) * cut(query)).astype(BF16),
            ]
        )

    pieces = [part(0)] + [swap(part(m), m) for m in range(1, ranks)]

    x_near = shift(jnp.stack([pieces[0][0], pieces[1][0]]), 1)
    y_near = shift(jnp.stack([pieces[0][1], pieces[1][1]]), -1)
    rate = lax.dynamic_slice_in_dim(pole_rate, q * local, local, 1).T / seq_total
    res = lax.dynamic_slice_in_dim(residues, q * local, local, 1).T
    med = lax.dynamic_slice_in_dim(med_filter, q * local, local, 0)
    root = jnp.sqrt(-jnp.expm1(-2.0 * rate))
    rate_wide = jnp.broadcast_to(rate[:, :, None], (local, GROUP, BLK))
    gain_wide = jnp.broadcast_to((res * root)[:, :, None], (local, GROUP, BLK))

    steps = local // STEP
    rows = STEP * GROUP

    def flat(value):
        return jnp.broadcast_to(value.reshape(steps, 1, BLK), (steps, 8, BLK))

    rate_row = flat(rate)
    root_row = flat(root)
    scale = 1.0 / math.sqrt(GROUP * seq_total)
    params = pltpu.CompilerParams(vmem_limit_bytes=8 << 20)
    smem = pl.BlockSpec(memory_space=pltpu.SMEM)
    whole = pl.BlockSpec(memory_space=pltpu.VMEM)

    def block(shape, axis, offset=0):
        def at(i):
            return tuple(i + offset if d == axis else 0 for d in range(len(shape)))

        return pl.BlockSpec(shape, at)

    def specs(offset=0):
        return dict(
            group=block((STEP, GROUP, BLK), 0, offset),
            row=block((1, 8, BLK), 0, offset),
            packed=block((1, GROUP, BLK), 0, offset),
            pair=block((2, rows, BLK), 1, offset),
            states=block((1, SPAN - 1, BLK, BLK), 0, offset),
            table=block((STEP, BLK, WIDE), 0, offset),
            lag=block((STEP, WIDE), 0, offset),
        )

    sp = specs()
    pieces[2], pieces[3], x_near, y_near, rate_row, root_row = lax.optimization_barrier(
        (pieces[2], pieces[3], x_near, y_near, rate_row, root_row)
    )
    x_far = shift(jnp.stack([pieces[2][0], pieces[3][0]]), 1)
    y_far = shift(jnp.stack([pieces[2][1], pieces[3][1]]), -1)

    table, rate_row = pl.pallas_call(
        table_kernel,
        grid=(steps,),
        in_specs=[sp["row"], sp["group"], sp["group"], block((STEP, SPAN * BLK), 0)],
        out_specs=[sp["table"], sp["row"]],
        out_shape=[
            jax.ShapeDtypeStruct((local, BLK, WIDE), BF16),
            jax.ShapeDtypeStruct(rate_row.shape, F32),
        ],
        compiler_params=params,
        name="tables",
    )(rate_row, rate_wide, gain_wide, med)

    store = jax.ShapeDtypeStruct((steps, SPAN - 1, BLK, BLK), BF16)
    small = jax.ShapeDtypeStruct((steps, GROUP, BLK), F32)
    blocks = pltpu.VMEM((2 * SPAN, rows, BLK), BF16)
    halo = (x_near, x_far, y_near, y_far)
    carried, returned, ends, ahead, behind, mail, cross = pl.pallas_call(
        state_kernel,
        grid=(steps,),
        in_specs=[smem, sp["group"], sp["row"]] + [sp["pair"]] * 8,
        out_specs=[sp["states"]] * 2 + [sp["packed"]] * 5,
        out_shape=[store] * 2 + [small] * 5,
        scratch_shapes=[blocks] * 2,
        compiler_params=params,
        name="states",
    )(q_arr, rate_wide, rate_row, *pieces, *halo)

    if units == 4:
        before = after = swap(mail, 2 * ranks)
    else:
        reach = 2
        while reach < units - 2:
            fade = jnp.exp(-rate_row[:, :1] * float(reach * ranks * length))
            ahead, behind = (
                ahead + fade * shift(ahead, reach),
                behind + fade * shift(behind, -reach),
            )
            reach *= 2
        before = shift(ahead, 2)
        after = shift(behind, -2)

    lag = pl.pallas_call(
        functools.partial(lag_kernel, scale=scale),
        grid=(steps,),
        in_specs=[smem, sp["group"], sp["row"], sp["row"], sp["packed"]] + [sp["pair"]] * 6,
        out_specs=sp["lag"],
        out_shape=jax.ShapeDtypeStruct((local, WIDE), F32),
        scratch_shapes=[
            pltpu.VMEM((SPAN, rows, BLK), BF16),
            blocks,
            pltpu.VMEM((STEP, 8, WIDE), F32),
        ],
        compiler_params=params,
        name="lags",
    )(q_arr, rate_wide, rate_row, root_row, cross, *pieces, y_near, y_far)
    before, after, lag = lax.optimization_barrier((before, after, lag))

    back = []
    parts = PARTS
    q_next = q_arr
    for h in range(parts):
        sh = specs(h * (steps // parts))
        so = specs()
        outs = pl.pallas_call(
            main_kernel,
            grid=(steps // parts,),
            in_specs=[smem, sh["group"], sh["group"], sh["row"], sh["table"]]
            + [sh["states"]] * 2
            + [sh["packed"]] * 2
            + [sh["pair"]] * 8,
            out_specs=[so["pair"]] * 4,
            out_shape=[jax.ShapeDtypeStruct((2, sub // parts, BLK), BF16)] * 4,
            scratch_shapes=[blocks] * 2 + [pltpu.VMEM((SPAN, rows, BLK), F32)] * 2,
            compiler_params=params,
            name="convs",
        )(
            q_next, rate_wide, gain_wide, rate_row, table, carried, returned, before, after,
            *pieces, *halo,
        )
        outs = list(outs)
        outs[0], q_next = lax.optimization_barrier((outs[0], q_arr))
        back += [outs[0]] + [swap(outs[m], m) for m in range(1, ranks)]

    back[0], lag = lax.optimization_barrier((back[0], lag))
    sums = pl.pallas_call(
        functools.partial(join_kernel, scale=scale),
        in_specs=[smem] + [whole] * 5,
        out_specs=whole,
        out_shape=jax.ShapeDtypeStruct((local, WIDE), F32),
        compiler_params=params,
        name="joins",
    )(q_arr, rate_row, root_row, ends, after, lag)

    hop = 1
    while hop < units:
        if hop == 2:
            back[4], sums = lax.optimization_barrier((back[4], sums))
        total = sums.astype(F32) + swap(sums, hop * ranks).astype(F32)
        sums = lax.reduce_precision(total, 8, 7).astype(BF16)
        hop *= 2
    back[2], back[3], sums = lax.optimization_barrier((back[2], back[3], sums))
    parts_of = [sums] + [swap(sums, m) for m in range(1, ranks)]

    grads = pl.pallas_call(
        gate_kernel,
        in_specs=[smem] + [whole] * (len(back) + 3),
        out_specs=[whole] * 3,
        out_shape=[jax.ShapeDtypeStruct((channels, length), BF16)] * 3,
        compiler_params=params,
        name="gates",
    )(q_arr, *back, grad_out, value_in, key_in)
    grad_med, grad_res = pl.pallas_call(
        sum_kernel,
        in_specs=[smem] + [whole] * ranks,
        out_specs=[whole] * 2,
        out_shape=[
            jax.ShapeDtypeStruct((groups, SPAN * BLK), F32),
            jax.ShapeDtypeStruct((GROUP, groups), F32),
        ],
        scratch_shapes=[pltpu.VMEM((groups, BLK), F32)],
        compiler_params=params,
        name="sums",
    )(q_arr, *parts_of)
    return (*grads, grad_med, grad_res)


def solution(mesh):
    in_specs = (
        P("ch", "ctx"),
        P("ch", "ctx"),
        P("ch", "ctx"),
        P("ch", "ctx"),
        P("ch", None),
        P(None, "ch"),
        P(None, "ch"),
    )
    out_specs = (P("ch", "ctx"), P("ch", "ctx"), P("ch", "ctx"), P("ch", None), P(None, "ch"))
    return jax.shard_map(body, mesh=mesh, in_specs=in_specs, out_specs=out_specs, check_vma=False)
```

```python
import functools
import math

import jax
import jax.numpy as jnp
from jax import lax
from jax.experimental import pallas as pl
from jax.experimental.pallas import tpu as pltpu
from jax.sharding import PartitionSpec as P

GROUP = 16
BLK = 128
SPAN = 4
STEP = 8
PARTS = 2
WIDE = (SPAN + 1) * BLK
F32 = jnp.float32
BF16 = jnp.bfloat16
NT = (((1,), (1,)), ((), ()))
TN = (((0,), (0,)), ((), ()))
NN = (((1,), (0,)), ((), ()))


def mm(left, right, dims=NN):
    return lax.dot_general(left, right, dims, preferred_element_type=F32)


def halves(value):
    high = value.astype(BF16)
    return high, (value - high.astype(F32)).astype(BF16)


def lanes_of(rows):
    return lax.broadcasted_iota(jnp.int32, (rows, BLK), 1)


def table_kernel(row_ref, rate_ref, gain_ref, med_ref, table_ref, next_ref):
    next_ref[...] = row_ref[...]
    lane = lanes_of(GROUP).astype(F32)
    for g in range(STEP):
        rate = rate_ref[g]
        gain = gain_ref[g]
        pieces = [jnp.zeros((1, BLK), F32)]
        for o in range(SPAN + 1):
            tail = jnp.sum(gain * jnp.exp(-rate * (lane + float(o * BLK))), axis=0, keepdims=True)
            if o < SPAN:
                tail = tail + med_ref[g : g + 1, o * BLK : (o + 1) * BLK].astype(F32)
            pieces.append(tail)
        taps = jnp.broadcast_to(jnp.concatenate(pieces, axis=1), (GROUP, WIDE + BLK))
        skewed = pltpu.roll(taps, 0, 1, stride=1, stride_axis=0)
        for i in range(BLK // GROUP):
            moved = skewed if i == 0 else pltpu.roll(skewed, GROUP * i, 1)
            table_ref[g, GROUP * i : GROUP * (i + 1), :] = moved[:, BLK:].astype(BF16)


def own_group(rows):
    row = lax.broadcasted_iota(jnp.int32, (rows, BLK), 0) // (rows // STEP)
    return row == lax.broadcasted_iota(jnp.int32, (rows, BLK), 1) // GROUP


def column_sum(value):
    total = value[0:GROUP]
    for g in range(1, STEP):
        total = total + value[GROUP * g : GROUP * (g + 1)]
    return total


def gather_blocks(q, pieces, near, far, xs, ys):
    for m, piece in enumerate(pieces):
        xs[SPAN + (q ^ m)] = piece[0]
        ys[q ^ m] = piece[1]
    for m in range(SPAN):
        x_part, y_part = near if m < 2 else far
        xs[q ^ m] = x_part[m % 2]
        ys[SPAN + (q ^ m)] = y_part[m % 2]


def state_kernel(
    q_ref, rate_ref, row_ref, p0, p1, p2, p3, xa, xb, ya, yb,
    car_ref, ret_ref, end_ref, ahead_ref, behind_ref, mail_ref, cross_ref, xs, ys,
):
    gather_blocks(q_ref[0] & 3, (p0, p1, p2, p3), (xa, ya), (xb, yb), xs, ys)
    rate = rate_ref[...].reshape(BLK, BLK)
    tok = lanes_of(BLK).astype(F32)
    row = row_ref[0, 0:1, :]
    decay = jnp.exp(-row * float(BLK))
    skip = jnp.exp(-row * float(SPAN * BLK))
    same = own_group(BLK)
    fin = jnp.concatenate(halves(jnp.exp(-rate * (BLK - 1.0 - tok))), axis=0)
    ini = jnp.concatenate(halves(jnp.exp(-rate * (tok + 1.0))), axis=0)

    def state(blocks, j, weights):
        both = mm(blocks[j], weights, NT)
        return jnp.where(same, both[:, :BLK] + both[:, BLK:], 0.0)

    carried = state(xs, 0, fin)
    for i in range(1, SPAN):
        car_ref[0, i - 1] = carried.astype(BF16)
        carried = carried * decay + state(xs, i, fin)
    own = [state(xs, SPAN + i, fin) for i in range(SPAN)]
    end = own[0]
    for i in range(1, SPAN):
        end = end * decay + own[i]
    end_ref[0] = column_sum(end)
    ahead = column_sum(end + skip * carried)
    ahead_ref[0] = ahead

    returned = state(ys, 2 * SPAN - 1, ini)
    cross = jnp.zeros((BLK, BLK), F32)
    for i in range(SPAN - 2, -1, -1):
        ret_ref[0, i] = returned.astype(BF16)
        cross = cross + own[i] * returned
        returned = returned * decay + state(ys, SPAN + i, ini)
    head = state(ys, SPAN - 1, ini)
    for i in range(SPAN - 2, -1, -1):
        head = head * decay + state(ys, i, ini)
    behind = column_sum(head + skip * returned)
    behind_ref[0] = behind
    mail_ref[0] = jnp.where((q_ref[0] & 4) > 0, ahead, behind)
    cross_ref[0] = column_sum(cross) * skip


def roll_left(value, amount):
    width = value.shape[1]
    return value if amount % width == 0 else pltpu.roll(value, width - amount, 1)


def fold(value):
    for step in (64, 32, 16):
        value = value + pltpu.roll(value, step, 1)
    return value


def lag_kernel(
    q_ref, rate_ref, row_ref, root_ref, cross_ref, p0, p1, p2, p3, ya, yb, lag_ref, xs, ys, sums,
    *, scale,
):
    q = q_ref[0] & 3
    for m, piece in enumerate((p0, p1, p2, p3)):
        xs[q ^ m] = piece[0]
        ys[q ^ m] = piece[1]
        ys[SPAN + (q ^ m)] = (ya if m < 2 else yb)[m % 2]
    row_at = lax.broadcasted_iota(jnp.int32, (BLK, BLK), 0)
    causal = lanes_of(BLK) >= row_at
    lane8 = lanes_of(8)
    for g in range(STEP):
        rows = slice(GROUP * g, GROUP * (g + 1))
        y = [ys[j, rows, :] for j in range(2 * SPAN)]
        wide_y = jnp.concatenate(
            [jnp.concatenate(y[o : o + SPAN], axis=0) for o in range(SPAN + 1)], axis=1
        )
        own_x = jnp.concatenate([xs[j, rows, :] for j in range(SPAN)], axis=0)
        pairs = mm(own_x, wide_y, TN)
        tiles = [pairs[:, o * BLK : (o + 1) * BLK] for o in range(SPAN + 1)]
        tiles[0] = jnp.where(causal, tiles[0], 0.0)
        count = BLK // 8
        parts = [[tile[8 * i : 8 * (i + 1)] for i in range(count)] for tile in tiles]
        while count > 1:
            count //= 2
            keep = lane8 < BLK - 8 * count
            moved = [
                [pltpu.roll(part[i + count], BLK - 8 * count, 1) for i in range(count)]
                for part in parts
            ]
            for o in range(SPAN + 1):
                for i in range(count):
                    after = moved[o + 1][i] if o < SPAN else 0.0
                    parts[o][i] = parts[o][i] + jnp.where(keep, moved[o][i], after)
        for o in range(SPAN + 1):
            sums[g, :, o * BLK : (o + 1) * BLK] = parts[o][0]
    lags = sums[:, 0, :]
    for r in range(1, 8):
        lags = lags + roll_left(sums[:, r, :], r)
    rate = rate_ref[...].reshape(BLK, BLK)
    row = row_ref[0, 0:1, :]
    fade = jnp.concatenate(halves(jnp.exp(-rate * lanes_of(BLK).astype(F32))), axis=0)
    split = jnp.concatenate(halves(lags), axis=0)
    coef = jnp.zeros((STEP, BLK), F32)
    for o in range(SPAN + 1):
        both = mm(split[:, o * BLK : (o + 1) * BLK], fade, NT)
        term = both[:STEP, :BLK] + both[:STEP, BLK:] + both[STEP:, :BLK]
        coef = coef + term * jnp.exp(-row * float(o * BLK))
    cross = jnp.sum(cross_ref[0], axis=0, keepdims=True)
    coef = fold(jnp.where(own_group(STEP), (coef + cross) * root_ref[0, 0:1, :], 0.0))
    lag_ref[...] = jnp.concatenate((lags[:, : SPAN * BLK], coef), axis=1) * scale


def join_kernel(q_ref, row_ref, root_ref, end_ref, after_ref, lag_ref, out_ref, *, scale):
    for step in range(row_ref.shape[0]):
        rows = slice(STEP * step, STEP * (step + 1))
        skip = jnp.exp(-row_ref[step, 0:1, :] * float(SPAN * BLK))
        cross = jnp.sum(end_ref[step] * after_ref[step], axis=0, keepdims=True)
        cross = cross * skip * root_ref[step, 0:1, :] * scale
        coef = fold(jnp.where(own_group(STEP) & ((q_ref[0] & 16) > 0), cross, 0.0))
        out_ref[rows, : SPAN * BLK] = lag_ref[rows, : SPAN * BLK]
        out_ref[rows, SPAN * BLK :] = lag_ref[rows, SPAN * BLK :] + coef


def main_kernel(
    q_ref, rate_ref, gain_ref, row_ref, table_ref, car_ref, ret_ref, before_ref, after_ref,
    p0, p1, p2, p3, xa, xb, ya, yb, o0, o1, o2, o3, xs, ys, fs, bs,
):
    q = q_ref[0] & 3
    gather_blocks(q, (p0, p1, p2, p3), (xa, ya), (xb, yb), xs, ys)
    rate = rate_ref[...].reshape(BLK, BLK)
    gain = gain_ref[...].reshape(BLK, BLK)
    tok = lanes_of(BLK).astype(F32)
    row = row_ref[0, 0:1, :]
    same = own_group(BLK)
    shift = float(SPAN * BLK)
    out_f = (gain * jnp.exp(-rate * (tok + 1.0 + shift))).astype(BF16)
    out_b = (gain * jnp.exp(-rate * (BLK - 1.0 - tok + shift))).astype(BF16)
    out_f = jnp.concatenate((out_f, out_f), axis=0)
    out_b = jnp.concatenate((out_b, out_b), axis=0)

    def spread(ref, flag):
        return jnp.where(same & (flag > 0), jnp.concatenate([ref[0]] * STEP, axis=0), 0.0)

    start = spread(before_ref, q_ref[0] & 8)
    stop = spread(after_ref, q_ref[0] & 16)
    none = jnp.zeros((BLK, BLK), BF16)
    far_f, far_b = [], []
    for i in range(SPAN):
        left = none if i == 0 else car_ref[0, i - 1]
        rest = (start * jnp.exp(-row * float(BLK * i))).astype(BF16)
        far_f.append(mm(jnp.concatenate((left, rest), axis=1), out_f))
        left = none if i == SPAN - 1 else ret_ref[0, i]
        rest = (stop * jnp.exp(-row * float(BLK * (SPAN - 1 - i)))).astype(BF16)
        far_b.append(mm(jnp.concatenate((left, rest), axis=1), out_b))
    for i in range(SPAN):
        fs[i] = far_f[i]
        bs[i] = far_b[i]
    for g in range(STEP):
        rows = slice(GROUP * g, GROUP * (g + 1))
        x = [xs[j, rows, :] for j in range(2 * SPAN)]
        y = [ys[j, rows, :] for j in range(2 * SPAN)]
        wide_x = jnp.concatenate(
            [jnp.concatenate(x[SPAN - o : 2 * SPAN - o], axis=0) for o in range(SPAN + 1)], axis=1
        )
        wide_y = jnp.concatenate(
            [jnp.concatenate(y[o : o + SPAN], axis=0) for o in range(SPAN + 1)], axis=1
        )
        table = table_ref[g]
        tall = jnp.concatenate(
            [table[:, o * BLK : (o + 1) * BLK] for o in range(SPAN + 1)], axis=0
        )
        forward = mm(wide_x, tall)
        backward = mm(wide_y, table, NT)
        for i in range(SPAN):
            cut = slice(GROUP * i, GROUP * (i + 1))
            fs[i, rows, :] += forward[cut]
            bs[i, rows, :] += backward[cut]
    for m, out in enumerate((o0, o1, o2, o3)):
        out[0] = fs[q ^ m].astype(BF16)
        out[1] = bs[q ^ m].astype(BF16)


def sum_kernel(q_ref, s0, s1, s2, s3, med_ref, res_ref, turned):
    q = q_ref[0] & 3
    local = s0.shape[0]
    for m, part in enumerate((s0, s1, s2, s3)):
        at = pl.ds(pl.multiple_of((q ^ m) * local, local), local)
        med_ref[at, :] = part[:, : SPAN * BLK].astype(F32)
        turned[at, :] = part[:, SPAN * BLK :].astype(F32)
    res_ref[...] = turned[...].T[:GROUP]


def gate_kernel(q_ref, *refs):
    q = q_ref[0] & 3
    pieces, (go_ref, v_ref, k_ref, gq_ref, gk_ref, gv_ref) = refs[:-6], refs[-6:]
    part = pieces[0].shape[1]
    parts = len(pieces) // SPAN
    for h in range(parts):
        for m in range(SPAN):
            piece = pieces[h * SPAN + m]
            at = pl.ds(pl.multiple_of((q ^ m) * (part * parts) + h * part, part), part)
            gq_ref[at, :] = (go_ref[at, :].astype(F32) * piece[0].astype(F32)).astype(BF16)
            grad = piece[1].astype(F32)
            gk_ref[at, :] = (grad * v_ref[at, :].astype(F32)).astype(BF16)
            gv_ref[at, :] = (grad * k_ref[at, :].astype(F32)).astype(BF16)


def body(query, key_in, value_in, grad_out, med_filter, residues, pole_rate):
    channels, length = query.shape
    groups = channels // GROUP
    devices = lax.axis_size("ctx")
    seq_total = length * devices
    ranks = SPAN
    units = devices // ranks
    sub = channels // ranks
    local = groups // ranks
    index = lax.axis_index("ctx")
    q = lax.rem(index, ranks).astype(jnp.int32)
    low = (index < 2 * ranks).astype(jnp.int32)
    one = jnp.int32(1)
    ahead_on, behind_on = (one - low, low) if units == 4 else (one, one)
    q_arr = (q + 4 * low + 8 * ahead_on + 16 * behind_on).reshape(1)

    def swap(value, m):
        return lax.ppermute(value, "ctx", [(i, i ^ m) for i in range(devices)])

    def shift(value, by):
        by = by * ranks
        return lax.ppermute(
            value, "ctx", [(i, i + by) for i in range(devices) if 0 <= i + by < devices]
        )

    def part(m):
        def cut(array):
            return lax.dynamic_slice_in_dim(array, (q ^ m) * sub, sub, 0).astype(F32)

        return jnp.stack(
            [
                (cut(key_in) * cut(value_in)).astype(BF16),
                (cut(grad_out) * cut(query)).astype(BF16),
            ]
        )

    pieces = [part(0)] + [swap(part(m), m) for m in range(1, ranks)]

    x_near = shift(jnp.stack([pieces[0][0], pieces[1][0]]), 1)
    y_near = shift(jnp.stack([pieces[0][1], pieces[1][1]]), -1)
    rate = lax.dynamic_slice_in_dim(pole_rate, q * local, local, 1).T / seq_total
    res = lax.dynamic_slice_in_dim(residues, q * local, local, 1).T
    med = lax.dynamic_slice_in_dim(med_filter, q * local, local, 0)
    root = jnp.sqrt(-jnp.expm1(-2.0 * rate))
    rate_wide = jnp.broadcast_to(rate[:, :, None], (local, GROUP, BLK))
    gain_wide = jnp.broadcast_to((res * root)[:, :, None], (local, GROUP, BLK))

    steps = local // STEP
    rows = STEP * GROUP

    def flat(value):
        return jnp.broadcast_to(value.reshape(steps, 1, BLK), (steps, 8, BLK))

    rate_row = flat(rate)
    root_row = flat(root)
    scale = 1.0 / math.sqrt(GROUP * seq_total)
    params = pltpu.CompilerParams(vmem_limit_bytes=24 << 20)
    smem = pl.BlockSpec(memory_space=pltpu.SMEM)
    whole = pl.BlockSpec(memory_space=pltpu.VMEM)

    def view(ref, kind, step):
        if kind == "all":
            return ref
        if kind == "pair":
            return ref.at[:, pl.ds(pl.multiple_of(step * rows, rows), rows), :]
        if kind == "one":
            return ref.at[pl.ds(step, 1)]
        return ref.at[pl.ds(pl.multiple_of(step * STEP, STEP), STEP)]

    def looped(kernel, kinds, count, name, out_shape, scratch=()):
        kinds = list(kinds) + [("all", 0)] * len(scratch)

        def whole_kernel(*refs):
            def turn(step, carry):
                kernel(*[view(ref, kind, step + at) for ref, (kind, at) in zip(refs, kinds)])
                return carry

            lax.fori_loop(0, count, turn, 0)

        ins = len(kinds) - len(scratch) - len(out_shape)
        return pl.pallas_call(
            whole_kernel,
            in_specs=[smem if kind == "all" else whole for kind, _ in kinds[:ins]],
            out_specs=[whole] * len(out_shape),
            out_shape=list(out_shape),
            scratch_shapes=list(scratch),
            compiler_params=params,
            name=name,
        )

    pieces[2], pieces[3], x_near, y_near, rate_row, root_row = lax.optimization_barrier(
        (pieces[2], pieces[3], x_near, y_near, rate_row, root_row)
    )
    x_far = shift(jnp.stack([pieces[2][0], pieces[3][0]]), 1)
    y_far = shift(jnp.stack([pieces[2][1], pieces[3][1]]), -1)

    few = ("few", 0)
    one = ("one", 0)
    pair = ("pair", 0)
    table, rate_row = looped(
        table_kernel,
        [one, few, few, few, few, one],
        steps,
        "tables",
        [
            jax.ShapeDtypeStruct((local, BLK, WIDE), BF16),
            jax.ShapeDtypeStruct(rate_row.shape, F32),
        ],
    )(rate_row, rate_wide, gain_wide, med)

    store = jax.ShapeDtypeStruct((steps, SPAN - 1, BLK, BLK), BF16)
    small = jax.ShapeDtypeStruct((steps, GROUP, BLK), F32)
    blocks = pltpu.VMEM((2 * SPAN, rows, BLK), BF16)
    halo = (x_near, x_far, y_near, y_far)
    carried, returned, ends, ahead, behind, mail, cross = looped(
        state_kernel,
        [("all", 0), few, one] + [pair] * 8 + [one] * 7,
        steps,
        "states",
        [store] * 2 + [small] * 5,
        [blocks] * 2,
    )(q_arr, rate_wide, rate_row, *pieces, *halo)

    if units == 4:
        before = after = swap(mail, 2 * ranks)
    else:
        reach = 2
        while reach < units - 2:
            fade = jnp.exp(-rate_row[:, :1] * float(reach * ranks * length))
            ahead, behind = (
                ahead + fade * shift(ahead, reach),
                behind + fade * shift(behind, -reach),
            )
            reach *= 2
        before = shift(ahead, 2)
        after = shift(behind, -2)

    (lag,) = looped(
        functools.partial(lag_kernel, scale=scale),
        [("all", 0), few, one, one, one] + [pair] * 6 + [few],
        steps,
        "lags",
        [jax.ShapeDtypeStruct((local, WIDE), F32)],
        [
            pltpu.VMEM((SPAN, rows, BLK), BF16),
            blocks,
            pltpu.VMEM((STEP, 8, WIDE), F32),
        ],
    )(q_arr, rate_wide, rate_row, root_row, cross, *pieces, y_near, y_far)
    before, after, lag = lax.optimization_barrier((before, after, lag))

    back = []
    parts = PARTS
    q_next = q_arr
    for h in range(parts):
        at = h * (steps // parts)
        outs = looped(
            main_kernel,
            [("all", 0)]
            + [(kind, at) for kind in ["few", "few", "one", "few"] + ["one"] * 4 + ["pair"] * 8]
            + [pair] * 4,
            steps // parts,
            "convs",
            [jax.ShapeDtypeStruct((2, sub // parts, BLK), BF16)] * 4,
            [blocks] * 2 + [pltpu.VMEM((SPAN, rows, BLK), F32)] * 2,
        )(
            q_next, rate_wide, gain_wide, rate_row, table, carried, returned, before, after,
            *pieces, *halo,
        )
        outs = list(outs)
        outs[0], q_next = lax.optimization_barrier((outs[0], q_arr))
        back += [outs[0]] + [swap(outs[m], m) for m in range(1, ranks)]

    back[0], lag = lax.optimization_barrier((back[0], lag))
    sums = pl.pallas_call(
        functools.partial(join_kernel, scale=scale),
        in_specs=[smem] + [whole] * 5,
        out_specs=whole,
        out_shape=jax.ShapeDtypeStruct((local, WIDE), F32),
        compiler_params=params,
        name="joins",
    )(q_arr, rate_row, root_row, ends, after, lag)

    hop = 1
    while hop < units:
        if hop == 2:
            back[4], sums = lax.optimization_barrier((back[4], sums))
        total = sums.astype(F32) + swap(sums, hop * ranks).astype(F32)
        sums = lax.reduce_precision(total, 8, 7).astype(BF16)
        hop *= 2
    back[2], back[3], sums = lax.optimization_barrier((back[2], back[3], sums))
    parts_of = [sums] + [swap(sums, m) for m in range(1, ranks)]

    grads = pl.pallas_call(
        gate_kernel,
        in_specs=[smem] + [whole] * (len(back) + 3),
        out_specs=[whole] * 3,
        out_shape=[jax.ShapeDtypeStruct((channels, length), BF16)] * 3,
        compiler_params=params,
        name="gates",
    )(q_arr, *back, grad_out, value_in, key_in)
    grad_med, grad_res = pl.pallas_call(
        sum_kernel,
        in_specs=[smem] + [whole] * ranks,
        out_specs=[whole] * 2,
        out_shape=[
            jax.ShapeDtypeStruct((groups, SPAN * BLK), F32),
            jax.ShapeDtypeStruct((GROUP, groups), F32),
        ],
        scratch_shapes=[pltpu.VMEM((groups, BLK), F32)],
        compiler_params=params,
        name="sums",
    )(q_arr, *parts_of)
    return (*grads, grad_med, grad_res)


def solution(mesh):
    in_specs = (
        P("ch", "ctx"),
        P("ch", "ctx"),
        P("ch", "ctx"),
        P("ch", "ctx"),
        P("ch", None),
        P(None, "ch"),
        P(None, "ch"),
    )
    out_specs = (P("ch", "ctx"), P("ch", "ctx"), P("ch", "ctx"), P("ch", None), P(None, "ch"))
    return jax.shard_map(body, mesh=mesh, in_specs=in_specs, out_specs=out_specs, check_vma=False)
```

```python
import functools
import math

import jax
import jax.numpy as jnp
from jax import lax
from jax.experimental import pallas as pl
from jax.experimental.pallas import tpu as pltpu
from jax.sharding import PartitionSpec as P

GROUP = 16
BLK = 128
SPAN = 4
STEP = 8
PARTS = 2
WIDE = (SPAN + 1) * BLK
F32 = jnp.float32
BF16 = jnp.bfloat16
NT = (((1,), (1,)), ((), ()))
TN = (((0,), (0,)), ((), ()))
NN = (((1,), (0,)), ((), ()))


def mm(left, right, dims=NN):
    return lax.dot_general(left, right, dims, preferred_element_type=F32)


def halves(value):
    high = value.astype(BF16)
    return high, (value - high.astype(F32)).astype(BF16)


def lanes_of(rows):
    return lax.broadcasted_iota(jnp.int32, (rows, BLK), 1)


def table_kernel(row_ref, rate_ref, gain_ref, med_ref, table_ref, next_ref):
    next_ref[...] = row_ref[...]
    lane = lanes_of(GROUP).astype(F32)
    for g in range(STEP):
        rate = rate_ref[g]
        gain = gain_ref[g]
        pieces = [jnp.zeros((1, BLK), F32)]
        for o in range(SPAN + 1):
            tail = jnp.sum(gain * jnp.exp(-rate * (lane + float(o * BLK))), axis=0, keepdims=True)
            if o < SPAN:
                tail = tail + med_ref[g : g + 1, o * BLK : (o + 1) * BLK].astype(F32)
            pieces.append(tail)
        taps = jnp.broadcast_to(jnp.concatenate(pieces, axis=1), (GROUP, WIDE + BLK))
        skewed = pltpu.roll(taps, 0, 1, stride=1, stride_axis=0)
        for i in range(BLK // GROUP):
            moved = skewed if i == 0 else pltpu.roll(skewed, GROUP * i, 1)
            table_ref[g, GROUP * i : GROUP * (i + 1), :] = moved[:, BLK:].astype(BF16)


def own_group(rows):
    row = lax.broadcasted_iota(jnp.int32, (rows, BLK), 0) // (rows // STEP)
    return row == lax.broadcasted_iota(jnp.int32, (rows, BLK), 1) // GROUP


def column_sum(value):
    total = value[0:GROUP]
    for g in range(1, STEP):
        total = total + value[GROUP * g : GROUP * (g + 1)]
    return total


def gather_blocks(q, pieces, near, two, three, xs, ys):
    for m, piece in enumerate(pieces):
        xs[SPAN + (q ^ m)] = piece[0]
        ys[q ^ m] = piece[1]
    for m in range(SPAN):
        x_part, y_part = (near, near, two, three)[m]
        xs[q ^ m] = x_part[m if m < 2 else 0]
        ys[SPAN + (q ^ m)] = y_part[m if m < 2 else 0]


def state_kernel(
    q_ref, rate_ref, row_ref, p0, p1, p2, p3, xa, xb, xc, ya, yb, yc,
    car_ref, ret_ref, end_ref, ahead_ref, behind_ref, mail_ref, cross_ref, xs, ys,
):
    gather_blocks(q_ref[0] & 3, (p0, p1, p2, p3), (xa, ya), (xb, yb), (xc, yc), xs, ys)
    rate = rate_ref[...].reshape(BLK, BLK)
    tok = lanes_of(BLK).astype(F32)
    row = row_ref[0, 0:1, :]
    decay = jnp.exp(-row * float(BLK))
    skip = jnp.exp(-row * float(SPAN * BLK))
    same = own_group(BLK)
    fin = jnp.concatenate(halves(jnp.exp(-rate * (BLK - 1.0 - tok))), axis=0)
    ini = jnp.concatenate(halves(jnp.exp(-rate * (tok + 1.0))), axis=0)

    def state(blocks, j, weights):
        both = mm(blocks[j], weights, NT)
        return jnp.where(same, both[:, :BLK] + both[:, BLK:], 0.0)

    carried = state(xs, 0, fin)
    for i in range(1, SPAN):
        car_ref[0, i - 1] = carried.astype(BF16)
        carried = carried * decay + state(xs, i, fin)
    own = [state(xs, SPAN + i, fin) for i in range(SPAN)]
    end = own[0]
    for i in range(1, SPAN):
        end = end * decay + own[i]
    end_ref[0] = column_sum(end)
    ahead = column_sum(end + skip * carried)
    ahead_ref[0] = ahead

    returned = state(ys, 2 * SPAN - 1, ini)
    cross = jnp.zeros((BLK, BLK), F32)
    for i in range(SPAN - 2, -1, -1):
        ret_ref[0, i] = returned.astype(BF16)
        cross = cross + own[i] * returned
        returned = returned * decay + state(ys, SPAN + i, ini)
    head = state(ys, SPAN - 1, ini)
    for i in range(SPAN - 2, -1, -1):
        head = head * decay + state(ys, i, ini)
    behind = column_sum(head + skip * returned)
    behind_ref[0] = behind
    mail_ref[0] = jnp.where((q_ref[0] & 4) > 0, ahead, behind)
    cross_ref[0] = column_sum(cross) * skip


def roll_left(value, amount):
    width = value.shape[1]
    return value if amount % width == 0 else pltpu.roll(value, width - amount, 1)


def fold(value):
    for step in (64, 32, 16):
        value = value + pltpu.roll(value, step, 1)
    return value


def lag_kernel(
    q_ref, rate_ref, row_ref, root_ref, cross_ref, p0, p1, p2, p3, ya, yb, yc, lag_ref, xs, ys, sums,
    *, scale,
):
    q = q_ref[0] & 3
    for m, piece in enumerate((p0, p1, p2, p3)):
        xs[q ^ m] = piece[0]
        ys[q ^ m] = piece[1]
        ys[SPAN + (q ^ m)] = (ya, ya, yb, yc)[m][m if m < 2 else 0]
    row_at = lax.broadcasted_iota(jnp.int32, (BLK, BLK), 0)
    causal = lanes_of(BLK) >= row_at
    lane8 = lanes_of(8)
    for g in range(STEP):
        rows = slice(GROUP * g, GROUP * (g + 1))
        y = [ys[j, rows, :] for j in range(2 * SPAN)]
        wide_y = jnp.concatenate(
            [jnp.concatenate(y[o : o + SPAN], axis=0) for o in range(SPAN + 1)], axis=1
        )
        own_x = jnp.concatenate([xs[j, rows, :] for j in range(SPAN)], axis=0)
        pairs = mm(own_x, wide_y, TN)
        tiles = [pairs[:, o * BLK : (o + 1) * BLK] for o in range(SPAN + 1)]
        tiles[0] = jnp.where(causal, tiles[0], 0.0)
        count = BLK // 8
        parts = [[tile[8 * i : 8 * (i + 1)] for i in range(count)] for tile in tiles]
        while count > 1:
            count //= 2
            keep = lane8 < BLK - 8 * count
            moved = [
                [pltpu.roll(part[i + count], BLK - 8 * count, 1) for i in range(count)]
                for part in parts
            ]
            for o in range(SPAN + 1):
                for i in range(count):
                    after = moved[o + 1][i] if o < SPAN else 0.0
                    parts[o][i] = parts[o][i] + jnp.where(keep, moved[o][i], after)
        for o in range(SPAN + 1):
            sums[g, :, o * BLK : (o + 1) * BLK] = parts[o][0]
    lags = sums[:, 0, :]
    for r in range(1, 8):
        lags = lags + roll_left(sums[:, r, :], r)
    rate = rate_ref[...].reshape(BLK, BLK)
    row = row_ref[0, 0:1, :]
    fade = jnp.concatenate(halves(jnp.exp(-rate * lanes_of(BLK).astype(F32))), axis=0)
    split = jnp.concatenate(halves(lags), axis=0)
    coef = jnp.zeros((STEP, BLK), F32)
    for o in range(SPAN + 1):
        both = mm(split[:, o * BLK : (o + 1) * BLK], fade, NT)
        term = both[:STEP, :BLK] + both[:STEP, BLK:] + both[STEP:, :BLK]
        coef = coef + term * jnp.exp(-row * float(o * BLK))
    cross = jnp.sum(cross_ref[0], axis=0, keepdims=True)
    coef = fold(jnp.where(own_group(STEP), (coef + cross) * root_ref[0, 0:1, :], 0.0))
    lag_ref[...] = jnp.concatenate((lags[:, : SPAN * BLK], coef), axis=1) * scale


def join_kernel(q_ref, row_ref, root_ref, end_ref, after_ref, lag_ref, out_ref, *, scale):
    for step in range(row_ref.shape[0]):
        rows = slice(STEP * step, STEP * (step + 1))
        skip = jnp.exp(-row_ref[step, 0:1, :] * float(SPAN * BLK))
        cross = jnp.sum(end_ref[step] * after_ref[step], axis=0, keepdims=True)
        cross = cross * skip * root_ref[step, 0:1, :] * scale
        coef = fold(jnp.where(own_group(STEP) & ((q_ref[0] & 16) > 0), cross, 0.0))
        out_ref[rows, : SPAN * BLK] = lag_ref[rows, : SPAN * BLK]
        out_ref[rows, SPAN * BLK :] = lag_ref[rows, SPAN * BLK :] + coef


def main_kernel(
    q_ref, rate_ref, gain_ref, row_ref, table_ref, car_ref, ret_ref, before_ref, after_ref,
    p0, p1, p2, p3, xa, xb, xc, ya, yb, yc, o0, o1, o2, o3, xs, ys, fs, bs,
):
    q = q_ref[0] & 3
    gather_blocks(q, (p0, p1, p2, p3), (xa, ya), (xb, yb), (xc, yc), xs, ys)
    rate = rate_ref[...].reshape(BLK, BLK)
    gain = gain_ref[...].reshape(BLK, BLK)
    tok = lanes_of(BLK).astype(F32)
    row = row_ref[0, 0:1, :]
    same = own_group(BLK)
    shift = float(SPAN * BLK)
    out_f = (gain * jnp.exp(-rate * (tok + 1.0 + shift))).astype(BF16)
    out_b = (gain * jnp.exp(-rate * (BLK - 1.0 - tok + shift))).astype(BF16)
    out_f = jnp.concatenate((out_f, out_f), axis=0)
    out_b = jnp.concatenate((out_b, out_b), axis=0)

    def spread(ref, flag):
        return jnp.where(same & (flag > 0), jnp.concatenate([ref[0]] * STEP, axis=0), 0.0)

    start = spread(before_ref, q_ref[0] & 8)
    stop = spread(after_ref, q_ref[0] & 16)
    none = jnp.zeros((BLK, BLK), BF16)
    far_f, far_b = [], []
    for i in range(SPAN):
        left = none if i == 0 else car_ref[0, i - 1]
        rest = (start * jnp.exp(-row * float(BLK * i))).astype(BF16)
        far_f.append(mm(jnp.concatenate((left, rest), axis=1), out_f))
        left = none if i == SPAN - 1 else ret_ref[0, i]
        rest = (stop * jnp.exp(-row * float(BLK * (SPAN - 1 - i)))).astype(BF16)
        far_b.append(mm(jnp.concatenate((left, rest), axis=1), out_b))
    for i in range(SPAN):
        fs[i] = far_f[i]
        bs[i] = far_b[i]
    for g in range(STEP):
        rows = slice(GROUP * g, GROUP * (g + 1))
        x = [xs[j, rows, :] for j in range(2 * SPAN)]
        y = [ys[j, rows, :] for j in range(2 * SPAN)]
        wide_x = jnp.concatenate(
            [jnp.concatenate(x[SPAN - o : 2 * SPAN - o], axis=0) for o in range(SPAN + 1)], axis=1
        )
        wide_y = jnp.concatenate(
            [jnp.concatenate(y[o : o + SPAN], axis=0) for o in range(SPAN + 1)], axis=1
        )
        table = table_ref[g]
        tall = jnp.concatenate(
            [table[:, o * BLK : (o + 1) * BLK] for o in range(SPAN + 1)], axis=0
        )
        forward = mm(wide_x, tall)
        backward = mm(wide_y, table, NT)
        for i in range(SPAN):
            cut = slice(GROUP * i, GROUP * (i + 1))
            fs[i, rows, :] += forward[cut]
            bs[i, rows, :] += backward[cut]
    for m, out in enumerate((o0, o1, o2, o3)):
        out[0] = fs[q ^ m].astype(BF16)
        out[1] = bs[q ^ m].astype(BF16)


def sum_kernel(q_ref, s0, s1, s2, s3, med_ref, res_ref, turned):
    q = q_ref[0] & 3
    local = s0.shape[0]
    for m, part in enumerate((s0, s1, s2, s3)):
        at = pl.ds(pl.multiple_of((q ^ m) * local, local), local)
        med_ref[at, :] = part[:, : SPAN * BLK].astype(F32)
        turned[at, :] = part[:, SPAN * BLK :].astype(F32)
    res_ref[...] = turned[...].T[:GROUP]


def gate_kernel(q_ref, *refs):
    q = q_ref[0] & 3
    pieces, (go_ref, v_ref, k_ref, gq_ref, gk_ref, gv_ref) = refs[:-6], refs[-6:]
    part = pieces[0].shape[1]
    parts = len(pieces) // SPAN
    for h in range(parts):
        for m in range(SPAN):
            piece = pieces[h * SPAN + m]
            at = pl.ds(pl.multiple_of((q ^ m) * (part * parts) + h * part, part), part)
            gq_ref[at, :] = (go_ref[at, :].astype(F32) * piece[0].astype(F32)).astype(BF16)
            grad = piece[1].astype(F32)
            gk_ref[at, :] = (grad * v_ref[at, :].astype(F32)).astype(BF16)
            gv_ref[at, :] = (grad * k_ref[at, :].astype(F32)).astype(BF16)


def body(query, key_in, value_in, grad_out, med_filter, residues, pole_rate):
    channels, length = query.shape
    groups = channels // GROUP
    devices = lax.axis_size("ctx")
    seq_total = length * devices
    ranks = SPAN
    units = devices // ranks
    sub = channels // ranks
    local = groups // ranks
    index = lax.axis_index("ctx")
    q = lax.rem(index, ranks).astype(jnp.int32)
    low = (index < 2 * ranks).astype(jnp.int32)
    one = jnp.int32(1)
    ahead_on, behind_on = (one - low, low) if units == 4 else (one, one)
    q_arr = (q + 4 * low + 8 * ahead_on + 16 * behind_on).reshape(1)

    def swap(value, m):
        return lax.ppermute(value, "ctx", [(i, i ^ m) for i in range(devices)])

    def shift(value, by):
        by = by * ranks
        return lax.ppermute(
            value, "ctx", [(i, i + by) for i in range(devices) if 0 <= i + by < devices]
        )

    def part(m):
        def cut(array):
            return lax.dynamic_slice_in_dim(array, (q ^ m) * sub, sub, 0).astype(F32)

        return jnp.stack(
            [
                (cut(key_in) * cut(value_in)).astype(BF16),
                (cut(grad_out) * cut(query)).astype(BF16),
            ]
        )

    mate, late = lax.optimization_barrier((swap(part(1), 1), part(2)))
    pieces = [part(0), mate, swap(late, 2), swap(part(3), 3)]

    x_near = shift(jnp.stack([pieces[0][0], pieces[1][0]]), 1)
    y_near = shift(jnp.stack([pieces[0][1], pieces[1][1]]), -1)
    rate = lax.dynamic_slice_in_dim(pole_rate, q * local, local, 1).T / seq_total
    res = lax.dynamic_slice_in_dim(residues, q * local, local, 1).T
    med = lax.dynamic_slice_in_dim(med_filter, q * local, local, 0)
    root = jnp.sqrt(-jnp.expm1(-2.0 * rate))
    rate_wide = jnp.broadcast_to(rate[:, :, None], (local, GROUP, BLK))
    gain_wide = jnp.broadcast_to((res * root)[:, :, None], (local, GROUP, BLK))

    steps = local // STEP
    rows = STEP * GROUP

    def flat(value):
        return jnp.broadcast_to(value.reshape(steps, 1, BLK), (steps, 8, BLK))

    rate_row = flat(rate)
    root_row = flat(root)
    scale = 1.0 / math.sqrt(GROUP * seq_total)
    params = pltpu.CompilerParams(vmem_limit_bytes=24 << 20)
    smem = pl.BlockSpec(memory_space=pltpu.SMEM)
    whole = pl.BlockSpec(memory_space=pltpu.VMEM)

    def view(ref, kind, step):
        if kind == "all":
            return ref
        if kind == "pair":
            return ref.at[:, pl.ds(pl.multiple_of(step * rows, rows), rows), :]
        if kind == "one":
            return ref.at[pl.ds(step, 1)]
        return ref.at[pl.ds(pl.multiple_of(step * STEP, STEP), STEP)]

    def looped(kernel, kinds, count, name, out_shape, scratch=()):
        kinds = list(kinds) + [("all", 0)] * len(scratch)

        def whole_kernel(*refs):
            def turn(step, carry):
                kernel(*[view(ref, kind, step + at) for ref, (kind, at) in zip(refs, kinds)])
                return carry

            lax.fori_loop(0, count, turn, 0)

        ins = len(kinds) - len(scratch) - len(out_shape)
        return pl.pallas_call(
            whole_kernel,
            in_specs=[smem if kind == "all" else whole for kind, _ in kinds[:ins]],
            out_specs=[whole] * len(out_shape),
            out_shape=list(out_shape),
            scratch_shapes=list(scratch),
            compiler_params=params,
            name=name,
        )

    x_three = shift(pieces[3][:1], 1)
    y_three = shift(pieces[3][1:], -1)
    pieces[2], x_near, y_near, rate_row, root_row = lax.optimization_barrier(
        (pieces[2], x_near, y_near, rate_row, root_row)
    )
    x_two = shift(pieces[2][:1], 1)
    y_two = shift(pieces[2][1:], -1)

    few = ("few", 0)
    one = ("one", 0)
    pair = ("pair", 0)
    table, rate_row = looped(
        table_kernel,
        [one, few, few, few, few, one],
        steps,
        "tables",
        [
            jax.ShapeDtypeStruct((local, BLK, WIDE), BF16),
            jax.ShapeDtypeStruct(rate_row.shape, F32),
        ],
    )(rate_row, rate_wide, gain_wide, med)

    store = jax.ShapeDtypeStruct((steps, SPAN - 1, BLK, BLK), BF16)
    small = jax.ShapeDtypeStruct((steps, GROUP, BLK), F32)
    blocks = pltpu.VMEM((2 * SPAN, rows, BLK), BF16)
    halo = (x_near, x_two, x_three, y_near, y_two, y_three)
    carried, returned, ends, ahead, behind, mail, cross = looped(
        state_kernel,
        [("all", 0), few, one] + [pair] * 10 + [one] * 7,
        steps,
        "states",
        [store] * 2 + [small] * 5,
        [blocks] * 2,
    )(q_arr, rate_wide, rate_row, *pieces, *halo)

    if units == 4:
        before = after = swap(mail, 2 * ranks)
    else:
        reach = 2
        while reach < units - 2:
            fade = jnp.exp(-rate_row[:, :1] * float(reach * ranks * length))
            ahead, behind = (
                ahead + fade * shift(ahead, reach),
                behind + fade * shift(behind, -reach),
            )
            reach *= 2
        before = shift(ahead, 2)
        after = shift(behind, -2)

    (lag,) = looped(
        functools.partial(lag_kernel, scale=scale),
        [("all", 0), few, one, one, one] + [pair] * 7 + [few],
        steps,
        "lags",
        [jax.ShapeDtypeStruct((local, WIDE), F32)],
        [
            pltpu.VMEM((SPAN, rows, BLK), BF16),
            blocks,
            pltpu.VMEM((STEP, 8, WIDE), F32),
        ],
    )(q_arr, rate_wide, rate_row, root_row, cross, *pieces, y_near, y_two, y_three)
    before, after, lag = lax.optimization_barrier((before, after, lag))

    back = []
    parts = PARTS
    q_next = q_arr
    for h in range(parts):
        at = h * (steps // parts)
        outs = looped(
            main_kernel,
            [("all", 0)]
            + [(kind, at) for kind in ["few", "few", "one", "few"] + ["one"] * 4 + ["pair"] * 10]
            + [pair] * 4,
            steps // parts,
            "convs",
            [jax.ShapeDtypeStruct((2, sub // parts, BLK), BF16)] * 4,
            [blocks] * 2 + [pltpu.VMEM((SPAN, rows, BLK), F32)] * 2,
        )(
            q_next, rate_wide, gain_wide, rate_row, table, carried, returned, before, after,
            *pieces, *halo,
        )
        outs = list(outs)
        back += [outs[0]] + [swap(outs[m], m) for m in range(1, ranks)]

    back[0], lag = lax.optimization_barrier((back[0], lag))
    sums = pl.pallas_call(
        functools.partial(join_kernel, scale=scale),
        in_specs=[smem] + [whole] * 5,
        out_specs=whole,
        out_shape=jax.ShapeDtypeStruct((local, WIDE), F32),
        compiler_params=params,
        name="joins",
    )(q_arr, rate_row, root_row, ends, after, lag)

    hop = 1
    while hop < units:
        if hop == 2:
            back[4], sums = lax.optimization_barrier((back[4], sums))
        total = sums.astype(F32) + swap(sums, hop * ranks).astype(F32)
        sums = lax.reduce_precision(total, 8, 7).astype(BF16)
        hop *= 2
    back[2], back[3], sums = lax.optimization_barrier((back[2], back[3], sums))
    parts_of = [sums] + [swap(sums, m) for m in range(1, ranks)]

    grads = pl.pallas_call(
        gate_kernel,
        in_specs=[smem] + [whole] * (len(back) + 3),
        out_specs=[whole] * 3,
        out_shape=[jax.ShapeDtypeStruct((channels, length), BF16)] * 3,
        compiler_params=params,
        name="gates",
    )(q_arr, *back, grad_out, value_in, key_in)
    grad_med, grad_res = pl.pallas_call(
        sum_kernel,
        in_specs=[smem] + [whole] * ranks,
        out_specs=[whole] * 2,
        out_shape=[
            jax.ShapeDtypeStruct((groups, SPAN * BLK), F32),
            jax.ShapeDtypeStruct((GROUP, groups), F32),
        ],
        scratch_shapes=[pltpu.VMEM((groups, BLK), F32)],
        compiler_params=params,
        name="sums",
    )(q_arr, *parts_of)
    return (*grads, grad_med, grad_res)


def solution(mesh):
    in_specs = (
        P("ch", "ctx"),
        P("ch", "ctx"),
        P("ch", "ctx"),
        P("ch", "ctx"),
        P("ch", None),
        P(None, "ch"),
        P(None, "ch"),
    )
    out_specs = (P("ch", "ctx"), P("ch", "ctx"), P("ch", "ctx"), P("ch", None), P(None, "ch"))
    return jax.shard_map(body, mesh=mesh, in_specs=in_specs, out_specs=out_specs, check_vma=False)
```

```python
import functools
import math

import jax
import jax.numpy as jnp
from jax import lax
from jax.experimental import pallas as pl
from jax.experimental.pallas import tpu as pltpu
from jax.sharding import PartitionSpec as P

GROUP = 16
BLK = 128
SPAN = 4
STEP = 8
PARTS = 2
WIDE = (SPAN + 1) * BLK
F32 = jnp.float32
BF16 = jnp.bfloat16
NT = (((1,), (1,)), ((), ()))
TN = (((0,), (0,)), ((), ()))
NN = (((1,), (0,)), ((), ()))


def mm(left, right, dims=NN):
    return lax.dot_general(left, right, dims, preferred_element_type=F32)


def halves(value):
    high = value.astype(BF16)
    return high, (value - high.astype(F32)).astype(BF16)


def lanes_of(rows):
    return lax.broadcasted_iota(jnp.int32, (rows, BLK), 1)


def table_kernel(row_ref, rate_ref, gain_ref, med_ref, table_ref, next_ref):
    next_ref[...] = row_ref[...]
    lane = lanes_of(GROUP).astype(F32)
    for g in range(STEP):
        rate = rate_ref[g]
        gain = gain_ref[g]
        pieces = [jnp.zeros((1, BLK), F32)]
        for o in range(SPAN + 1):
            tail = jnp.sum(gain * jnp.exp(-rate * (lane + float(o * BLK))), axis=0, keepdims=True)
            if o < SPAN:
                tail = tail + med_ref[g : g + 1, o * BLK : (o + 1) * BLK].astype(F32)
            pieces.append(tail)
        taps = jnp.broadcast_to(jnp.concatenate(pieces, axis=1), (GROUP, WIDE + BLK))
        skewed = pltpu.roll(taps, 0, 1, stride=1, stride_axis=0)
        for i in range(BLK // GROUP):
            moved = skewed if i == 0 else pltpu.roll(skewed, GROUP * i, 1)
            table_ref[g, GROUP * i : GROUP * (i + 1), :] = moved[:, BLK:].astype(BF16)


def own_group(rows):
    row = lax.broadcasted_iota(jnp.int32, (rows, BLK), 0) // (rows // STEP)
    return row == lax.broadcasted_iota(jnp.int32, (rows, BLK), 1) // GROUP


def column_sum(value):
    total = value[0:GROUP]
    for g in range(1, STEP):
        total = total + value[GROUP * g : GROUP * (g + 1)]
    return total


def gather_blocks(q, pieces, near, two, three, xs, ys):
    for m, piece in enumerate(pieces):
        xs[SPAN + (q ^ m)] = piece[0]
        ys[q ^ m] = piece[1]
    for m in range(SPAN):
        x_part, y_part = (near, near, two, three)[m]
        xs[q ^ m] = x_part[m if m < 2 else 0]
        ys[SPAN + (q ^ m)] = y_part[m if m < 2 else 0]


def state_kernel(
    q_ref, rate_ref, row_ref, p0, p1, p2, p3, xa, xb, xc, ya, yb, yc,
    car_ref, ret_ref, end_ref, ahead_ref, behind_ref, mail_ref, cross_ref, xs, ys,
):
    gather_blocks(q_ref[0] & 3, (p0, p1, p2, p3), (xa, ya), (xb, yb), (xc, yc), xs, ys)
    rate = rate_ref[...].reshape(BLK, BLK)
    tok = lanes_of(BLK).astype(F32)
    row = row_ref[0, 0:1, :]
    decay = jnp.exp(-row * float(BLK))
    skip = jnp.exp(-row * float(SPAN * BLK))
    same = own_group(BLK)
    fin = jnp.concatenate(halves(jnp.exp(-rate * (BLK - 1.0 - tok))), axis=0)
    ini = jnp.concatenate(halves(jnp.exp(-rate * (tok + 1.0))), axis=0)

    def state(blocks, j, weights):
        both = mm(blocks[j], weights, NT)
        return jnp.where(same, both[:, :BLK] + both[:, BLK:], 0.0)

    carried = state(xs, 0, fin)
    for i in range(1, SPAN):
        car_ref[0, i - 1] = carried.astype(BF16)
        carried = carried * decay + state(xs, i, fin)
    own = [state(xs, SPAN + i, fin) for i in range(SPAN)]
    end = own[0]
    for i in range(1, SPAN):
        end = end * decay + own[i]
    end_ref[0] = column_sum(end)
    ahead = column_sum(end + skip * carried)
    ahead_ref[0] = ahead

    returned = state(ys, 2 * SPAN - 1, ini)
    cross = jnp.zeros((BLK, BLK), F32)
    for i in range(SPAN - 2, -1, -1):
        ret_ref[0, i] = returned.astype(BF16)
        cross = cross + own[i] * returned
        returned = returned * decay + state(ys, SPAN + i, ini)
    head = state(ys, SPAN - 1, ini)
    for i in range(SPAN - 2, -1, -1):
        head = head * decay + state(ys, i, ini)
    behind = column_sum(head + skip * returned)
    behind_ref[0] = behind
    mail_ref[0] = jnp.where((q_ref[0] & 4) > 0, ahead, behind)
    cross_ref[0] = column_sum(cross) * skip


def roll_left(value, amount):
    width = value.shape[1]
    return value if amount % width == 0 else pltpu.roll(value, width - amount, 1)


def fold(value):
    for step in (64, 32, 16):
        value = value + pltpu.roll(value, step, 1)
    return value


def lag_kernel(
    q_ref, rate_ref, row_ref, root_ref, cross_ref, p0, p1, p2, p3, ya, yb, yc, lag_ref, xs, ys, sums,
    *, scale,
):
    q = q_ref[0] & 3
    for m, piece in enumerate((p0, p1, p2, p3)):
        xs[q ^ m] = piece[0]
        ys[q ^ m] = piece[1]
        ys[SPAN + (q ^ m)] = (ya, ya, yb, yc)[m][m if m < 2 else 0]
    row_at = lax.broadcasted_iota(jnp.int32, (BLK, BLK), 0)
    causal = lanes_of(BLK) >= row_at
    lane8 = lanes_of(8)
    for g in range(STEP):
        rows = slice(GROUP * g, GROUP * (g + 1))
        y = [ys[j, rows, :] for j in range(2 * SPAN)]
        wide_y = jnp.concatenate(
            [jnp.concatenate(y[o : o + SPAN], axis=0) for o in range(SPAN + 1)], axis=1
        )
        own_x = jnp.concatenate([xs[j, rows, :] for j in range(SPAN)], axis=0)
        moved = roll_left(wide_y, 64)
        last = jnp.where(lanes_of(SPAN * GROUP) < 64, moved[:, SPAN * BLK :], 0.0).astype(BF16)
        moved = jnp.concatenate((moved[:, : SPAN * BLK], last), axis=1)
        tall = jnp.concatenate((own_x[:, :64], pltpu.roll(own_x, 64, 1)[:, :64]), axis=0)
        pairs = mm(tall, jnp.concatenate((wide_y, moved), axis=0), TN)
        tiles = [pairs[:, o * BLK : (o + 1) * BLK] for o in range(SPAN + 1)]
        tiles[0] = jnp.where(causal[:64], tiles[0], 0.0)
        count = 8
        parts = [[tile[8 * i : 8 * (i + 1)] for i in range(count)] for tile in tiles]
        while count > 1:
            count //= 2
            keep = lane8 < BLK - 8 * count
            moved = [
                [pltpu.roll(part[i + count], BLK - 8 * count, 1) for i in range(count)]
                for part in parts
            ]
            for o in range(SPAN + 1):
                for i in range(count):
                    after = moved[o + 1][i] if o < SPAN else 0.0
                    parts[o][i] = parts[o][i] + jnp.where(keep, moved[o][i], after)
        for o in range(SPAN + 1):
            sums[g, :, o * BLK : (o + 1) * BLK] = parts[o][0]
    lags = sums[:, 0, :]
    for r in range(1, 8):
        lags = lags + roll_left(sums[:, r, :], r)
    rate = rate_ref[...].reshape(BLK, BLK)
    row = row_ref[0, 0:1, :]
    fade = jnp.concatenate(halves(jnp.exp(-rate * lanes_of(BLK).astype(F32))), axis=0)
    split = jnp.concatenate(halves(lags), axis=0)
    coef = jnp.zeros((STEP, BLK), F32)
    for o in range(SPAN + 1):
        both = mm(split[:, o * BLK : (o + 1) * BLK], fade, NT)
        term = both[:STEP, :BLK] + both[:STEP, BLK:] + both[STEP:, :BLK]
        coef = coef + term * jnp.exp(-row * float(o * BLK))
    cross = jnp.sum(cross_ref[0], axis=0, keepdims=True)
    coef = fold(jnp.where(own_group(STEP), (coef + cross) * root_ref[0, 0:1, :], 0.0))
    lag_ref[...] = jnp.concatenate((lags[:, : SPAN * BLK], coef), axis=1) * scale


def join_kernel(q_ref, row_ref, root_ref, end_ref, after_ref, lag_ref, out_ref, *, scale):
    for step in range(row_ref.shape[0]):
        rows = slice(STEP * step, STEP * (step + 1))
        skip = jnp.exp(-row_ref[step, 0:1, :] * float(SPAN * BLK))
        cross = jnp.sum(end_ref[step] * after_ref[step], axis=0, keepdims=True)
        cross = cross * skip * root_ref[step, 0:1, :] * scale
        coef = fold(jnp.where(own_group(STEP) & ((q_ref[0] & 16) > 0), cross, 0.0))
        out_ref[rows, : SPAN * BLK] = lag_ref[rows, : SPAN * BLK]
        out_ref[rows, SPAN * BLK :] = lag_ref[rows, SPAN * BLK :] + coef


def main_kernel(
    q_ref, rate_ref, gain_ref, row_ref, table_ref, car_ref, ret_ref, before_ref, after_ref,
    p0, p1, p2, p3, xa, xb, xc, ya, yb, yc, o0, o1, o2, o3, xs, ys, fs, bs,
):
    q = q_ref[0] & 3
    gather_blocks(q, (p0, p1, p2, p3), (xa, ya), (xb, yb), (xc, yc), xs, ys)
    rate = rate_ref[...].reshape(BLK, BLK)
    gain = gain_ref[...].reshape(BLK, BLK)
    tok = lanes_of(BLK).astype(F32)
    row = row_ref[0, 0:1, :]
    same = own_group(BLK)
    shift = float(SPAN * BLK)
    out_f = (gain * jnp.exp(-rate * (tok + 1.0 + shift))).astype(BF16)
    out_b = (gain * jnp.exp(-rate * (BLK - 1.0 - tok + shift))).astype(BF16)
    out_f = jnp.concatenate((out_f, out_f), axis=0)
    out_b = jnp.concatenate((out_b, out_b), axis=0)

    def spread(ref, flag):
        return jnp.where(same & (flag > 0), jnp.concatenate([ref[0]] * STEP, axis=0), 0.0)

    start = spread(before_ref, q_ref[0] & 8)
    stop = spread(after_ref, q_ref[0] & 16)
    none = jnp.zeros((BLK, BLK), BF16)
    far_f, far_b = [], []
    for i in range(SPAN):
        left = none if i == 0 else car_ref[0, i - 1]
        rest = (start * jnp.exp(-row * float(BLK * i))).astype(BF16)
        far_f.append(mm(jnp.concatenate((left, rest), axis=1), out_f))
        left = none if i == SPAN - 1 else ret_ref[0, i]
        rest = (stop * jnp.exp(-row * float(BLK * (SPAN - 1 - i)))).astype(BF16)
        far_b.append(mm(jnp.concatenate((left, rest), axis=1), out_b))
    for i in range(SPAN):
        fs[i] = far_f[i]
        bs[i] = far_b[i]
    for g in range(STEP):
        rows = slice(GROUP * g, GROUP * (g + 1))
        x = [xs[j, rows, :] for j in range(2 * SPAN)]
        y = [ys[j, rows, :] for j in range(2 * SPAN)]
        wide_x = jnp.concatenate(
            [jnp.concatenate(x[SPAN - o : 2 * SPAN - o], axis=0) for o in range(SPAN + 1)], axis=1
        )
        wide_y = jnp.concatenate(
            [jnp.concatenate(y[o : o + SPAN], axis=0) for o in range(SPAN + 1)], axis=1
        )
        table = table_ref[g]
        tall = jnp.concatenate(
            [table[:, o * BLK : (o + 1) * BLK] for o in range(SPAN + 1)], axis=0
        )
        forward = mm(wide_x, tall)
        backward = mm(wide_y, table, NT)
        for i in range(SPAN):
            cut = slice(GROUP * i, GROUP * (i + 1))
            fs[i, rows, :] += forward[cut]
            bs[i, rows, :] += backward[cut]
    for m, out in enumerate((o0, o1, o2, o3)):
        out[0] = fs[q ^ m].astype(BF16)
        out[1] = bs[q ^ m].astype(BF16)


def sum_kernel(q_ref, s0, s1, s2, s3, med_ref, res_ref, turned):
    q = q_ref[0] & 3
    local = s0.shape[0]
    for m, part in enumerate((s0, s1, s2, s3)):
        at = pl.ds(pl.multiple_of((q ^ m) * local, local), local)
        med_ref[at, :] = part[:, : SPAN * BLK].astype(F32)
        turned[at, :] = part[:, SPAN * BLK :].astype(F32)
    res_ref[...] = turned[...].T[:GROUP]


def gate_kernel(q_ref, *refs):
    q = q_ref[0] & 3
    pieces, (go_ref, v_ref, k_ref, gq_ref, gk_ref, gv_ref) = refs[:-6], refs[-6:]
    part = pieces[0].shape[1]
    parts = len(pieces) // SPAN
    for h in range(parts):
        for m in range(SPAN):
            piece = pieces[h * SPAN + m]
            at = pl.ds(pl.multiple_of((q ^ m) * (part * parts) + h * part, part), part)
            gq_ref[at, :] = (go_ref[at, :].astype(F32) * piece[0].astype(F32)).astype(BF16)
            grad = piece[1].astype(F32)
            gk_ref[at, :] = (grad * v_ref[at, :].astype(F32)).astype(BF16)
            gv_ref[at, :] = (grad * k_ref[at, :].astype(F32)).astype(BF16)


def body(query, key_in, value_in, grad_out, med_filter, residues, pole_rate):
    channels, length = query.shape
    groups = channels // GROUP
    devices = lax.axis_size("ctx")
    seq_total = length * devices
    ranks = SPAN
    units = devices // ranks
    sub = channels // ranks
    local = groups // ranks
    index = lax.axis_index("ctx")
    q = lax.rem(index, ranks).astype(jnp.int32)
    low = (index < 2 * ranks).astype(jnp.int32)
    one = jnp.int32(1)
    ahead_on, behind_on = (one - low, low) if units == 4 else (one, one)
    q_arr = (q + 4 * low + 8 * ahead_on + 16 * behind_on).reshape(1)

    def swap(value, m):
        return lax.ppermute(value, "ctx", [(i, i ^ m) for i in range(devices)])

    def shift(value, by):
        by = by * ranks
        return lax.ppermute(
            value, "ctx", [(i, i + by) for i in range(devices) if 0 <= i + by < devices]
        )

    def part(m):
        def cut(array):
            return lax.dynamic_slice_in_dim(array, (q ^ m) * sub, sub, 0).astype(F32)

        return jnp.stack(
            [
                (cut(key_in) * cut(value_in)).astype(BF16),
                (cut(grad_out) * cut(query)).astype(BF16),
            ]
        )

    mate, late = lax.optimization_barrier((swap(part(1), 1), part(2)))
    pieces = [part(0), mate, swap(late, 2), swap(part(3), 3)]

    x_near = shift(jnp.stack([pieces[0][0], pieces[1][0]]), 1)
    y_near = shift(jnp.stack([pieces[0][1], pieces[1][1]]), -1)
    rate = lax.dynamic_slice_in_dim(pole_rate, q * local, local, 1).T / seq_total
    res = lax.dynamic_slice_in_dim(residues, q * local, local, 1).T
    med = lax.dynamic_slice_in_dim(med_filter, q * local, local, 0)
    root = jnp.sqrt(-jnp.expm1(-2.0 * rate))
    rate_wide = jnp.broadcast_to(rate[:, :, None], (local, GROUP, BLK))
    gain_wide = jnp.broadcast_to((res * root)[:, :, None], (local, GROUP, BLK))

    steps = local // STEP
    rows = STEP * GROUP

    def flat(value):
        return jnp.broadcast_to(value.reshape(steps, 1, BLK), (steps, 8, BLK))

    rate_row = flat(rate)
    root_row = flat(root)
    scale = 1.0 / math.sqrt(GROUP * seq_total)
    params = pltpu.CompilerParams(vmem_limit_bytes=24 << 20)
    smem = pl.BlockSpec(memory_space=pltpu.SMEM)
    whole = pl.BlockSpec(memory_space=pltpu.VMEM)

    def view(ref, kind, step):
        if kind == "all":
            return ref
        if kind == "pair":
            return ref.at[:, pl.ds(pl.multiple_of(step * rows, rows), rows), :]
        if kind == "one":
            return ref.at[pl.ds(step, 1)]
        return ref.at[pl.ds(pl.multiple_of(step * STEP, STEP), STEP)]

    def looped(kernel, kinds, count, name, out_shape, scratch=()):
        kinds = list(kinds) + [("all", 0)] * len(scratch)

        def whole_kernel(*refs):
            def turn(step, carry):
                kernel(*[view(ref, kind, step + at) for ref, (kind, at) in zip(refs, kinds)])
                return carry

            lax.fori_loop(0, count, turn, 0)

        ins = len(kinds) - len(scratch) - len(out_shape)
        return pl.pallas_call(
            whole_kernel,
            in_specs=[smem if kind == "all" else whole for kind, _ in kinds[:ins]],
            out_specs=[whole] * len(out_shape),
            out_shape=list(out_shape),
            scratch_shapes=list(scratch),
            compiler_params=params,
            name=name,
        )

    x_three = shift(pieces[3][:1], 1)
    y_three = shift(pieces[3][1:], -1)
    pieces[2], x_near, y_near, rate_row, root_row = lax.optimization_barrier(
        (pieces[2], x_near, y_near, rate_row, root_row)
    )
    x_two = shift(pieces[2][:1], 1)
    y_two = shift(pieces[2][1:], -1)

    few = ("few", 0)
    one = ("one", 0)
    pair = ("pair", 0)
    table, rate_row = looped(
        table_kernel,
        [one, few, few, few, few, one],
        steps,
        "tables",
        [
            jax.ShapeDtypeStruct((local, BLK, WIDE), BF16),
            jax.ShapeDtypeStruct(rate_row.shape, F32),
        ],
    )(rate_row, rate_wide, gain_wide, med)

    store = jax.ShapeDtypeStruct((steps, SPAN - 1, BLK, BLK), BF16)
    small = jax.ShapeDtypeStruct((steps, GROUP, BLK), F32)
    blocks = pltpu.VMEM((2 * SPAN, rows, BLK), BF16)
    halo = (x_near, x_two, x_three, y_near, y_two, y_three)
    carried, returned, ends, ahead, behind, mail, cross = looped(
        state_kernel,
        [("all", 0), few, one] + [pair] * 10 + [one] * 7,
        steps,
        "states",
        [store] * 2 + [small] * 5,
        [blocks] * 2,
    )(q_arr, rate_wide, rate_row, *pieces, *halo)

    if units == 4:
        before = after = swap(mail, 2 * ranks)
    else:
        reach = 2
        while reach < units - 2:
            fade = jnp.exp(-rate_row[:, :1] * float(reach * ranks * length))
            ahead, behind = (
                ahead + fade * shift(ahead, reach),
                behind + fade * shift(behind, -reach),
            )
            reach *= 2
        before = shift(ahead, 2)
        after = shift(behind, -2)

    (lag,) = looped(
        functools.partial(lag_kernel, scale=scale),
        [("all", 0), few, one, one, one] + [pair] * 7 + [few],
        steps,
        "lags",
        [jax.ShapeDtypeStruct((local, WIDE), F32)],
        [
            pltpu.VMEM((SPAN, rows, BLK), BF16),
            blocks,
            pltpu.VMEM((STEP, 8, WIDE), F32),
        ],
    )(q_arr, rate_wide, rate_row, root_row, cross, *pieces, y_near, y_two, y_three)
    before, after, lag = lax.optimization_barrier((before, after, lag))

    back = []
    parts = PARTS
    q_next = q_arr
    for h in range(parts):
        at = h * (steps // parts)
        outs = looped(
            main_kernel,
            [("all", 0)]
            + [(kind, at) for kind in ["few", "few", "one", "few"] + ["one"] * 4 + ["pair"] * 10]
            + [pair] * 4,
            steps // parts,
            "convs",
            [jax.ShapeDtypeStruct((2, sub // parts, BLK), BF16)] * 4,
            [blocks] * 2 + [pltpu.VMEM((SPAN, rows, BLK), F32)] * 2,
        )(
            q_next, rate_wide, gain_wide, rate_row, table, carried, returned, before, after,
            *pieces, *halo,
        )
        outs = list(outs)
        back += [outs[0]] + [swap(outs[m], m) for m in range(1, ranks)]

    back[0], lag = lax.optimization_barrier((back[0], lag))
    sums = pl.pallas_call(
        functools.partial(join_kernel, scale=scale),
        in_specs=[smem] + [whole] * 5,
        out_specs=whole,
        out_shape=jax.ShapeDtypeStruct((local, WIDE), F32),
        compiler_params=params,
        name="joins",
    )(q_arr, rate_row, root_row, ends, after, lag)

    hop = 1
    while hop < units:
        if hop == 2:
            back[4], sums = lax.optimization_barrier((back[4], sums))
        total = sums.astype(F32) + swap(sums, hop * ranks).astype(F32)
        sums = lax.reduce_precision(total, 8, 7).astype(BF16)
        hop *= 2
    back[2], back[3], sums = lax.optimization_barrier((back[2], back[3], sums))
    parts_of = [sums] + [swap(sums, m) for m in range(1, ranks)]

    grads = pl.pallas_call(
        gate_kernel,
        in_specs=[smem] + [whole] * (len(back) + 3),
        out_specs=[whole] * 3,
        out_shape=[jax.ShapeDtypeStruct((channels, length), BF16)] * 3,
        compiler_params=params,
        name="gates",
    )(q_arr, *back, grad_out, value_in, key_in)
    grad_med, grad_res = pl.pallas_call(
        sum_kernel,
        in_specs=[smem] + [whole] * ranks,
        out_specs=[whole] * 2,
        out_shape=[
            jax.ShapeDtypeStruct((groups, SPAN * BLK), F32),
            jax.ShapeDtypeStruct((GROUP, groups), F32),
        ],
        scratch_shapes=[pltpu.VMEM((groups, BLK), F32)],
        compiler_params=params,
        name="sums",
    )(q_arr, *parts_of)
    return (*grads, grad_med, grad_res)


def solution(mesh):
    in_specs = (
        P("ch", "ctx"),
        P("ch", "ctx"),
        P("ch", "ctx"),
        P("ch", "ctx"),
        P("ch", None),
        P(None, "ch"),
        P(None, "ch"),
    )
    out_specs = (P("ch", "ctx"), P("ch", "ctx"), P("ch", "ctx"), P("ch", None), P(None, "ch"))
    return jax.shard_map(body, mesh=mesh, in_specs=in_specs, out_specs=out_specs, check_vma=False)
```
